32 devices in a mesh: sec: 4 (over y, x), col: 8 (over z, core).
Axes of the slice: x: 2, y: 2, z: 4, core: 2. Of those that a mesh axis runs over, the one named last changes fastest.
Arguments:
- matrix_rows: float32 [4096, 16384], P('sec', 'col'), may hold values from -6 to 6
- factor_bank: float32 [4, 8, 512, 512], P(None, 'sec', 'col'), may hold values from -1 to 1, as said below
- owner_table: int32 [4, 8, 8], P(None, 'sec'), may hold values from 0 to 7, each once within a row
Outputs:
- updated: float32 [4096, 16384], P('sec', 'col')
The draws below stay inside these ranges and needn't reach their ends.
Inputs may be any that keep to these rules, and one draw needn't show every extreme that they name: `factor_bank`: each factor G[r,k] is orthogonal. `owner_table`: for each round and section the list names every row block once.
All inputs are finite; a program needn't handle non-finite values.
Results may differ from the reference program's by a relative error of at most 0.00014.
Values sent between devices are 32-bit elements; how exact they have to be, the bound alone decides.
A program may use at most 128 MiB of HBM per device.

```python
import jax
import jax.numpy as jnp
from jax import lax

F = 512
ROUNDS = 4
SECTIONS = 8
ROWS = 4096
CUT = 16384
N_COL = 8


def draw_factor_bank(key, part):
    raw = jax.random.normal(key, (ROUNDS, SECTIONS, F, F), jnp.float32)
    orthogonal, upper = jnp.linalg.qr(raw)
    return orthogonal


def level_of(stream_key, shape, split, low, largest):
    loudness, own = 1.0, jax.random.fold_in(stream_key, 6)
    for dim, shards_of in split:
        draws = jnp.exp(jax.random.uniform(jax.random.fold_in(own, dim), (shards_of,), jnp.float32, low / len(split), largest / len(split)))
        loudness = loudness * jnp.repeat(draws, shape[dim] // shards_of).reshape([-1 if axis == dim else 1 for axis in range(len(shape))])
    return loudness


def centred(stream_key, dims, deviation, most, pieces=(), held_as=jnp.bfloat16):
    array = jax.random.normal(stream_key, dims, jnp.float32) * deviation
    if len(pieces) > 0:
        array = level_of(stream_key, dims, pieces, -0.22, 0.18) * array
    return jnp.clip(array, min=-most, max=most).astype(held_as)


def setup_inputs(seed: int = 0) -> dict:
    seeds = jax.random.split(jax.random.key(seed), 4)
    matrix_rows = centred(seeds[0], (ROWS, CUT), 1.0, 6.0, ((0, 4), (1, 8)), jnp.float32)
    factor_bank = draw_factor_bank(jax.random.fold_in(seeds[3], 71), 0)
    owner_table = jax.vmap(lambda own: jax.random.permutation(own, N_COL))(jax.random.split(seeds[2], ROUNDS * SECTIONS)).reshape((ROUNDS, SECTIONS, N_COL)).astype(jnp.int32)
    return {"matrix_rows": matrix_rows, "factor_bank": factor_bank, "owner_table": owner_table}


def assemble(stored, owner_now):
    sections = stored.shape[0]
    extent = stored.shape[1]
    groups = owner_now.shape[1]
    blocks = stored.reshape(sections, groups, extent // groups, extent)
    labels = jnp.arange(groups, dtype=jnp.int32)
    onehot = (owner_now[:, :, None] == labels[None, None, :]).astype(stored.dtype)
    placed = jnp.einsum('scb,scnf->sbnf', onehot, blocks, precision=lax.Precision.HIGHEST)
    return placed.reshape(sections, extent, extent)

def reference(matrix_rows, factor_bank, owner_table):
    current = matrix_rows
    for number in range(ROUNDS):
        factors = assemble(factor_bank[number], owner_table[number])
        if number % 2 == 1:
            current = jnp.roll(current, F // 2, axis=0)
        windows = current.reshape(SECTIONS, F, -1)
        current = lax.map(lambda couple: jnp.dot(couple[0], couple[1], precision=lax.Precision.HIGHEST), (factors, windows))
        current = current.reshape(SECTIONS * F, -1)
        if number % 2 == 1:
            current = jnp.roll(current, -(F // 2), axis=0)
    return current
```

```python
import functools

import jax
import jax.numpy as jnp
from jax import lax
from jax.experimental import pallas as pl
from jax.experimental.pallas import tpu as pltpu
from jax.sharding import PartitionSpec as P

ROUNDS = 4
WIDTH = 256
PIECES = 2


def unit_order(sections):
    order = []
    for number in range(ROUNDS):
        ks = list(range(sections))
        if number % 2 == 0:
            ks = ks[::-1]
        order += [(number, k) for k in ks]
    return order


def strip_kernel(nsec, count, chunks, width, *refs):
    table_ref, x_ref, bank_ref, out_ref = refs[:4]
    xs, sa, sb, rs, ghi, glo = refs[4:10]
    sections = bank_ref.shape[1]
    order = unit_order(sections)
    units = len(order)
    held = refs[10 : 10 + units]
    (x_sems, o_sems, own_sems, up_sems, down_sems, piece_sems, far_sems, relay_sems, row_sems) = refs[10 + units :]

    extent = bank_ref.shape[3]
    half = extent // 2
    rows = bank_ref.shape[2]
    local_rows = sections * extent
    chips = count // 2
    sec = lax.axis_index("sec")
    me = lax.axis_index("col")
    chip, core = me // 2, me % 2
    partner = chip * 2 + 1 - core
    after = lax.rem(sec + 1, nsec)
    before = lax.rem(sec + nsec - 1, nsec)

    def columns(c):
        return pl.ds(pl.multiple_of(c * width, width), width)

    def load(c, k):
        return pltpu.make_async_copy(
            x_ref.at[pl.ds(k * extent, extent), columns(c)],
            xs.at[c, pl.ds(half + k * extent, extent)],
            x_sems.at[k, c],
        )

    def own(u):
        number, k = order[u]
        return pltpu.make_async_copy(bank_ref.at[number, k], held[u].at[core, chip], own_sems.at[u])

    for k in range(sections - 1, -1, -1):
        lax.fori_loop(0, chunks, lambda c, _, k=k: (load(c, k).start(), 0)[1], 0)
    for u in range(units):
        own(u).start()

    barrier = pltpu.get_barrier_semaphore()

    def greet(target):
        pl.semaphore_signal(barrier, inc=1, device_id=target, device_id_type=pl.DeviceIdType.MESH)

    greet({"col": partner})
    for d in range(1, chips):
        greet({"col": lax.rem(chip + d, chips) * 2 + core})
    greet({"sec": after})
    greet({"sec": before})
    pl.semaphore_wait(barrier, chips + 2)

    def remote(src, dst, sems, at, target):
        return pltpu.make_async_remote_copy(
            src_ref=src,
            dst_ref=dst,
            send_sem=sems.at[(0, *at)],
            recv_sem=sems.at[(1, *at)],
            device_id=target,
            device_id_type=pl.DeviceIdType.MESH,
        )

    part = rows // PIECES
    first_number, first_k = order[0]

    def piece(p):
        return pl.ds(p * part, part)

    def pass_up(src, slot, step, p):
        return remote(src, held[0].at[core, slot, piece(p)], up_sems, (step, p), {"col": (chip + 1) * 2 + core})

    def pass_down(src, slot, step, p):
        return remote(src, held[0].at[core, slot, piece(p)], down_sems, (step, p), {"col": (chip - 1) * 2 + core})

    def pass_pair(src, slot, step, p):
        return remote(src, held[0].at[core, slot, piece(p)], piece_sems, (step, p), {"col": partner})

    def own_piece(p):
        return bank_ref.at[first_number, first_k, piece(p)]

    has_up, has_down = chip + 1 < chips, chip > 0
    for p in range(PIECES):
        pl.when(has_up)(lambda p=p: pass_up(own_piece(p), chip, 0, p).start())
        pl.when(has_down)(lambda p=p: pass_down(own_piece(p), chip, 0, p).start())
    for p in range(PIECES):
        pass_pair(own_piece(p), chip, 0, p).start()
    for step in range(chips - 1):
        low, high = chip - 1 - step, chip + 1 + step
        for p in range(PIECES):

            @pl.when(low >= 0)
            def _(step=step, p=p, low=low):
                src = held[0].at[core, low, piece(p)]
                pass_up(src, low, step, p).wait_recv()
                if step + 1 < chips - 1:
                    pl.when(has_up)(lambda: pass_up(src, low, step + 1, p).start())
                pass_pair(src, low, 1 + step, p).start()

            @pl.when(high < chips)
            def _(step=step, p=p, high=high):
                src = held[0].at[core, high, piece(p)]
                pass_down(src, high, step, p).wait_recv()
                if step + 1 < chips - 1:
                    pl.when(has_down)(lambda: pass_down(src, high, step + 1, p).start())
                pass_pair(src, high, chips + step, p).start()

    def far(u, d):
        number, k = order[u]
        return remote(
            bank_ref.at[number, k],
            held[u].at[core, chip],
            far_sems,
            (u, d - 1),
            {"col": lax.rem(chip + d, chips) * 2 + core},
        )

    def far_arrival(u, d):
        return remote(
            bank_ref.at[order[u]],
            held[u].at[core, lax.rem(chip + chips - d, chips)],
            far_sems,
            (u, d - 1),
            {"col": partner},
        )

    def relay(u, side):
        return remote(held[u].at[side], held[u].at[side], relay_sems, (u,), {"col": partner})

    def order_rows(u):
        number, k = order[u]
        for b in range(count):
            place = jnp.int32(0)
            for c in range(count):
                place = jnp.where(table_ref[number, k, c] == b, c, place)
            block = held[u][place % 2, place // 2]
            high = block.astype(jnp.bfloat16)
            ghi[u, b * rows : (b + 1) * rows, :] = high
            glo[u, b * rows : (b + 1) * rows, :] = (block - high.astype(jnp.float32)).astype(jnp.bfloat16)

    own(0).wait()
    for step in range(chips - 1):
        low, high = chip - 1 - step, chip + 1 + step
        for p in range(PIECES):
            pl.when(low >= 0)(
                lambda: pass_pair(held[0].at[1 - core, low, piece(p)], low, 1 + step, p).wait_recv()
            )
            pl.when(high < chips)(
                lambda: pass_pair(held[0].at[1 - core, high, piece(p)], high, chips + step, p).wait_recv()
            )
    for p in range(PIECES):
        pass_pair(held[0].at[1 - core, chip, piece(p)], chip, 0, p).wait_recv()
    order_rows(0)

    def receive(u):
        for d in range(1, chips):
            far_arrival(u, d).wait_recv()
        own(u).wait()
        relay(u, core).start()
        relay(u, 1 - core).wait_recv()
        order_rows(u)

    def split(value):
        high = value.astype(jnp.bfloat16)
        return high, (value - high.astype(jnp.float32)).astype(jnp.bfloat16)

    def product(u, begin, size, parts):
        high, low = parts
        a, b = ghi[u, begin : begin + size, :], glo[u, begin : begin + size, :]
        dot = functools.partial(jnp.dot, preferred_element_type=jnp.float32)
        return dot(a, high) + (dot(a, low) + dot(b, high))

    index = {pair: u for u, pair in enumerate(order)}
    top = half + local_rows

    def forward(c, which, buf):
        return remote(
            buf.at[c, pl.ds(top - half, half)], buf.at[c, pl.ds(0, half)], row_sems, (which, c), {"sec": after}
        )

    def back_first(c):
        return remote(rs.at[c], sb.at[c, pl.ds(local_rows - half, half)], row_sems, (1, c), {"sec": before})

    def back_last(c):
        return remote(
            sa.at[c, pl.ds(0, half)],
            out_ref.at[pl.ds(local_rows - half, half), columns(c)],
            row_sems,
            (3, c),
            {"sec": before},
        )

    def each_chunk(body):
        lax.fori_loop(0, chunks, lambda c, _: (body(c), 0)[1], 0)

    last = sections - 1

    def begin(c):
        load(c, last).wait()
        parts = split(xs[c, half + last * extent : top])
        u = index[0, last]
        sa[c, top - half : top] = product(u, half, half, parts)
        forward(c, 0, sa).start()
        sa[c, half + last * extent : top - half] = product(u, 0, half, parts)

    each_chunk(begin)
    for u in range(1, units):
        for d in range(1, chips):
            far(u, d).start()

    for k in range(last - 1, -1, -1):
        receive(index[0, k])

        def inner(c, k=k):
            load(c, k).wait()
            at = half + k * extent
            parts = split(xs[c, at : at + extent])
            sa[c, at : at + extent] = product(index[0, k], 0, extent, parts)

        each_chunk(inner)

    receive(index[1, 0])

    def straddle(c):
        forward(c, 0, sa).wait_recv()
        parts = split(sa[c, 0:extent])
        u = index[1, 0]
        rs[c] = product(u, 0, half, parts)
        back_first(c).start()
        sb[c, 0:half] = product(u, half, half, parts)

    each_chunk(straddle)
    for k in range(1, sections):
        receive(index[1, k])

        def inner(c, k=k):
            parts = split(sa[c, k * extent : (k + 1) * extent])
            sb[c, k * extent - half : (k + 1) * extent - half] = product(index[1, k], 0, extent, parts)

        each_chunk(inner)

    for k in range(last, -1, -1):
        receive(index[2, k])

    def middle(c):
        back_first(c).wait_recv()
        parts = split(sb[c, last * extent : local_rows])
        u = index[2, last]
        xs[c, top - half : top] = product(u, half, half, parts)
        forward(c, 2, xs).start()
        xs[c, half + last * extent : top - half] = product(u, 0, half, parts)
        for k in range(last):
            at = half + k * extent
            parts = split(sb[c, k * extent : (k + 1) * extent])
            xs[c, at : at + extent] = product(index[2, k], 0, extent, parts)

    each_chunk(middle)

    for k in range(sections):
        receive(index[3, k])

    def store(c):
        return pltpu.make_async_copy(
            sa.at[c, pl.ds(half, local_rows - half)],
            out_ref.at[pl.ds(0, local_rows - half), columns(c)],
            o_sems.at[c],
        )

    def finish(c):
        forward(c, 2, xs).wait_recv()
        forward(c, 0, sa).wait_send()
        parts = split(xs[c, 0:extent])
        u = index[3, 0]
        sa[c, 0:half] = product(u, 0, half, parts)
        back_last(c).start()
        sa[c, half:extent] = product(u, half, half, parts)
        for k in range(1, sections):
            parts = split(xs[c, k * extent : (k + 1) * extent])
            sa[c, k * extent : (k + 1) * extent] = product(index[3, k], 0, extent, parts)
        store(c).start()

    each_chunk(finish)

    def drain(c):
        back_first(c).wait_send()
        forward(c, 2, xs).wait_send()
        store(c).wait()
        back_last(c).wait_send()
        back_last(c).wait_recv()

    for p in range(PIECES):
        pass_pair(own_piece(p), chip, 0, p).wait_send()
        pl.when(has_up)(lambda p=p: pass_up(own_piece(p), chip, 0, p).wait_send())
        pl.when(has_down)(lambda p=p: pass_down(own_piece(p), chip, 0, p).wait_send())
        for step in range(chips - 1):
            low, high = chip - 1 - step, chip + 1 + step

            @pl.when(low >= 0)
            def _():
                if step + 1 < chips - 1:
                    pl.when(has_up)(lambda: pass_up(held[0].at[core, low, piece(p)], low, step + 1, p).wait_send())
                pass_pair(held[0].at[core, low, piece(p)], low, 1 + step, p).wait_send()

            @pl.when(high < chips)
            def _():
                if step + 1 < chips - 1:
                    pl.when(has_down)(
                        lambda: pass_down(held[0].at[core, high, piece(p)], high, step + 1, p).wait_send()
                    )
                pass_pair(held[0].at[core, high, piece(p)], high, chips + step, p).wait_send()

    for u in range(1, units):
        for d in range(1, chips):
            far(u, d).wait_send()
        relay(u, core).wait_send()
    each_chunk(drain)


def local(matrix_rows, factor_bank, owner_table):
    nsec, count = lax.axis_size("sec"), lax.axis_size("col")
    sections, rows, extent = factor_bank.shape[1:]
    local_rows, columns = matrix_rows.shape
    half, chips = extent // 2, count // 2
    width = WIDTH if columns % WIDTH == 0 else columns
    chunks = columns // width
    units = ROUNDS * sections
    f32, bf16, dma = jnp.float32, jnp.bfloat16, pltpu.SemaphoreType.DMA
    return pl.pallas_call(
        functools.partial(strip_kernel, nsec, count, chunks, width),
        out_shape=jax.ShapeDtypeStruct(matrix_rows.shape, matrix_rows.dtype),
        in_specs=[
            pl.BlockSpec(memory_space=pltpu.SMEM),
            pl.BlockSpec(memory_space=pl.ANY),
            pl.BlockSpec(memory_space=pl.ANY),
        ],
        out_specs=pl.BlockSpec(memory_space=pl.ANY),
        scratch_shapes=[
            pltpu.VMEM((chunks, half + local_rows, width), f32),
            pltpu.VMEM((chunks, half + local_rows, width), f32),
            pltpu.VMEM((chunks, local_rows, width), f32),
            pltpu.VMEM((chunks, half, width), f32),
            pltpu.VMEM((units, extent, extent), bf16),
            pltpu.VMEM((units, extent, extent), bf16),
            *[pltpu.VMEM((2, chips, rows, extent), f32) for _ in range(units)],
            dma((sections, chunks)),
            dma((chunks,)),
            dma((units,)),
            dma((2, chips - 1, PIECES)),
            dma((2, chips - 1, PIECES)),
            dma((2, 2 * chips - 1, PIECES)),
            dma((2, units, chips - 1)),
            dma((2, units)),
            dma((2, 4, chunks)),
        ],
        compiler_params=pltpu.CompilerParams(
            collective_id=0, has_side_effects=True, vmem_limit_bytes=60 << 20
        ),
        name="strip",
    )(owner_table, matrix_rows, factor_bank)


def solution(mesh):
    in_specs = (P("sec", "col"), P(None, "sec", "col", None), P(None, "sec", None))
    out_specs = P("sec", "col")
    return jax.shard_map(local, mesh=mesh, in_specs=in_specs, out_specs=out_specs, check_vma=False)
```

```python
import functools

import jax
import jax.numpy as jnp
from jax import lax
from jax.experimental import pallas as pl
from jax.experimental.pallas import tpu as pltpu
from jax.sharding import PartitionSpec as P

ROUNDS = 4
WIDTH = 256
PIECES = 2


def unit_order(sections):
    order = []
    for number in range(ROUNDS):
        ks = list(range(sections))
        if number % 2 == 0:
            ks = ks[::-1]
        order += [(number, k) for k in ks]
    return order


def strip_kernel(nsec, count, chunks, width, *refs):
    table_ref, x_ref, bank_ref, out_ref = refs[:4]
    xs, sa, sb, rs, ghi, glo = refs[4:10]
    sections = bank_ref.shape[1]
    order = unit_order(sections)
    units = len(order)
    held = refs[10 : 10 + units]
    (x_sems, own_sems, up_sems, down_sems, piece_sems, far_sems, relay_sems, row_sems) = refs[10 + units :]

    extent = bank_ref.shape[3]
    half = extent // 2
    rows = bank_ref.shape[2]
    local_rows = sections * extent
    chips = count // 2
    sec = lax.axis_index("sec")
    me = lax.axis_index("col")
    chip, core = me // 2, me % 2
    partner = chip * 2 + 1 - core
    after = lax.rem(sec + 1, nsec)
    before = lax.rem(sec + nsec - 1, nsec)

    def columns(c):
        return pl.ds(pl.multiple_of(c * width, width), width)

    def load(c, k):
        return pltpu.make_async_copy(
            x_ref.at[pl.ds(k * extent, extent), columns(c)],
            xs.at[c, pl.ds(half + k * extent, extent)],
            x_sems.at[k, c],
        )

    def own(u):
        number, k = order[u]
        return pltpu.make_async_copy(bank_ref.at[number, k], held[u].at[core, chip], own_sems.at[u])

    for k in range(sections - 1, -1, -1):
        lax.fori_loop(0, chunks, lambda c, _, k=k: (load(c, k).start(), 0)[1], 0)
    for u in range(units):
        own(u).start()

    barrier = pltpu.get_barrier_semaphore()

    def greet(target):
        pl.semaphore_signal(barrier, inc=1, device_id=target, device_id_type=pl.DeviceIdType.MESH)

    greet({"col": partner})
    for d in range(1, chips):
        greet({"col": lax.rem(chip + d, chips) * 2 + core})
    greet({"sec": after})
    greet({"sec": before})
    pl.semaphore_wait(barrier, chips + 2)

    def remote(src, dst, sems, at, target):
        return pltpu.make_async_remote_copy(
            src_ref=src,
            dst_ref=dst,
            send_sem=sems.at[(0, *at)],
            recv_sem=sems.at[(1, *at)],
            device_id=target,
            device_id_type=pl.DeviceIdType.MESH,
        )

    part = rows // PIECES
    first_number, first_k = order[0]

    def piece(p):
        return pl.ds(p * part, part)

    def pass_up(src, slot, step, p):
        return remote(src, held[0].at[core, slot, piece(p)], up_sems, (step, p), {"col": (chip + 1) * 2 + core})

    def pass_down(src, slot, step, p):
        return remote(src, held[0].at[core, slot, piece(p)], down_sems, (step, p), {"col": (chip - 1) * 2 + core})

    def pass_pair(src, slot, step, p):
        return remote(src, held[0].at[core, slot, piece(p)], piece_sems, (step, p), {"col": partner})

    def own_piece(p):
        return bank_ref.at[first_number, first_k, piece(p)]

    has_up, has_down = chip + 1 < chips, chip > 0
    for p in range(PIECES):
        pl.when(has_up)(lambda p=p: pass_up(own_piece(p), chip, 0, p).start())
        pl.when(has_down)(lambda p=p: pass_down(own_piece(p), chip, 0, p).start())
    for p in range(PIECES):
        pass_pair(own_piece(p), chip, 0, p).start()
    for step in range(chips - 1):
        low, high = chip - 1 - step, chip + 1 + step
        for p in range(PIECES):

            @pl.when(low >= 0)
            def _(step=step, p=p, low=low):
                src = held[0].at[core, low, piece(p)]
                pass_up(src, low, step, p).wait_recv()
                if step + 1 < chips - 1:
                    pl.when(has_up)(lambda: pass_up(src, low, step + 1, p).start())
                pass_pair(src, low, 1 + step, p).start()

            @pl.when(high < chips)
            def _(step=step, p=p, high=high):
                src = held[0].at[core, high, piece(p)]
                pass_down(src, high, step, p).wait_recv()
                if step + 1 < chips - 1:
                    pl.when(has_down)(lambda: pass_down(src, high, step + 1, p).start())
                pass_pair(src, high, chips + step, p).start()

    def far(u, d):
        number, k = order[u]
        return remote(
            bank_ref.at[number, k],
            held[u].at[core, chip],
            far_sems,
            (u, d - 1),
            {"col": lax.rem(chip + d, chips) * 2 + core},
        )

    def far_arrival(u, d):
        return remote(
            bank_ref.at[order[u]],
            held[u].at[core, lax.rem(chip + chips - d, chips)],
            far_sems,
            (u, d - 1),
            {"col": partner},
        )

    def relay(u, side):
        return remote(held[u].at[side], held[u].at[side], relay_sems, (u,), {"col": partner})

    def order_rows(u):
        number, k = order[u]
        for b in range(count):
            place = jnp.int32(0)
            for c in range(count):
                place = jnp.where(table_ref[number, k, c] == b, c, place)
            block = held[u][place % 2, place // 2]
            high = block.astype(jnp.bfloat16)
            ghi[u, b * rows : (b + 1) * rows, :] = high
            glo[u, b * rows : (b + 1) * rows, :] = (block - high.astype(jnp.float32)).astype(jnp.bfloat16)

    own(0).wait()
    for step in range(chips - 1):
        low, high = chip - 1 - step, chip + 1 + step
        for p in range(PIECES):
            pl.when(low >= 0)(
                lambda: pass_pair(held[0].at[1 - core, low, piece(p)], low, 1 + step, p).wait_recv()
            )
            pl.when(high < chips)(
                lambda: pass_pair(held[0].at[1 - core, high, piece(p)], high, chips + step, p).wait_recv()
            )
    for p in range(PIECES):
        pass_pair(held[0].at[1 - core, chip, piece(p)], chip, 0, p).wait_recv()
    order_rows(0)

    def receive(u):
        for d in range(1, chips):
            far_arrival(u, d).wait_recv()
        own(u).wait()
        relay(u, core).start()
        relay(u, 1 - core).wait_recv()
        order_rows(u)

    def split(value):
        high = value.astype(jnp.bfloat16)
        return high, (value - high.astype(jnp.float32)).astype(jnp.bfloat16)

    def product(u, begin, size, parts):
        high, low = parts
        a, b = ghi[u, begin : begin + size, :], glo[u, begin : begin + size, :]
        dot = functools.partial(jnp.dot, preferred_element_type=jnp.float32)
        return dot(a, high) + (dot(a, low) + dot(b, high))

    index = {pair: u for u, pair in enumerate(order)}
    top = half + local_rows

    def forward(c, which, buf):
        return remote(
            buf.at[c, pl.ds(top - half, half)], buf.at[c, pl.ds(0, half)], row_sems, (which, c), {"sec": after}
        )

    def back_first(c):
        return remote(rs.at[c], sb.at[c, pl.ds(local_rows - half, half)], row_sems, (1, c), {"sec": before})

    def back_last(c):
        return remote(
            sa.at[c, pl.ds(0, half)],
            out_ref.at[pl.ds(local_rows - half, half), columns(c)],
            row_sems,
            (3, c),
            {"sec": before},
        )

    def each_chunk(body):
        lax.fori_loop(0, chunks, lambda c, _: (body(c), 0)[1], 0)

    last = sections - 1

    def begin(c):
        load(c, last).wait()
        parts = split(xs[c, half + last * extent : top])
        u = index[0, last]
        sa[c, top - half : top] = product(u, half, half, parts)
        forward(c, 0, sa).start()
        sa[c, half + last * extent : top - half] = product(u, 0, half, parts)

    each_chunk(begin)
    for u in range(1, units):
        for d in range(1, chips):
            far(u, d).start()

    for k in range(last - 1, -1, -1):
        receive(index[0, k])

        def inner(c, k=k):
            load(c, k).wait()
            at = half + k * extent
            parts = split(xs[c, at : at + extent])
            sa[c, at : at + extent] = product(index[0, k], 0, extent, parts)

        each_chunk(inner)

    receive(index[1, 0])

    def straddle(c):
        forward(c, 0, sa).wait_recv()
        parts = split(sa[c, 0:extent])
        u = index[1, 0]
        rs[c] = product(u, 0, half, parts)
        back_first(c).start()
        sb[c, 0:half] = product(u, half, half, parts)

    each_chunk(straddle)
    for k in range(1, sections):
        receive(index[1, k])

        def inner(c, k=k):
            parts = split(sa[c, k * extent : (k + 1) * extent])
            sb[c, k * extent - half : (k + 1) * extent - half] = product(index[1, k], 0, extent, parts)

        each_chunk(inner)

    for k in range(last, -1, -1):
        receive(index[2, k])

    def middle(c):
        back_first(c).wait_recv()
        parts = split(sb[c, last * extent : local_rows])
        u = index[2, last]
        xs[c, top - half : top] = product(u, half, half, parts)
        forward(c, 2, xs).start()
        xs[c, half + last * extent : top - half] = product(u, 0, half, parts)
        for k in range(last):
            at = half + k * extent
            parts = split(sb[c, k * extent : (k + 1) * extent])
            xs[c, at : at + extent] = product(index[2, k], 0, extent, parts)

    each_chunk(middle)

    for k in range(sections):
        receive(index[3, k])

    def finish(c):
        forward(c, 2, xs).wait_recv()
        parts = split(xs[c, 0:extent])
        u = index[3, 0]
        sa[c, 0:half] = product(u, 0, half, parts)
        back_last(c).start()
        out_ref[0:half, columns(c)] = product(u, half, half, parts)
        for k in range(1, sections):
            parts = split(xs[c, k * extent : (k + 1) * extent])
            out_ref[k * extent - half : (k + 1) * extent - half, columns(c)] = product(
                index[3, k], 0, extent, parts
            )

    each_chunk(finish)

    def drain(c):
        forward(c, 0, sa).wait_send()
        back_first(c).wait_send()
        forward(c, 2, xs).wait_send()
        back_last(c).wait_send()
        back_last(c).wait_recv()

    for p in range(PIECES):
        pass_pair(own_piece(p), chip, 0, p).wait_send()
        pl.when(has_up)(lambda p=p: pass_up(own_piece(p), chip, 0, p).wait_send())
        pl.when(has_down)(lambda p=p: pass_down(own_piece(p), chip, 0, p).wait_send())
        for step in range(chips - 1):
            low, high = chip - 1 - step, chip + 1 + step

            @pl.when(low >= 0)
            def _():
                if step + 1 < chips - 1:
                    pl.when(has_up)(lambda: pass_up(held[0].at[core, low, piece(p)], low, step + 1, p).wait_send())
                pass_pair(held[0].at[core, low, piece(p)], low, 1 + step, p).wait_send()

            @pl.when(high < chips)
            def _():
                if step + 1 < chips - 1:
                    pl.when(has_down)(
                        lambda: pass_down(held[0].at[core, high, piece(p)], high, step + 1, p).wait_send()
                    )
                pass_pair(held[0].at[core, high, piece(p)], high, chips + step, p).wait_send()

    for u in range(1, units):
        for d in range(1, chips):
            far(u, d).wait_send()
        relay(u, core).wait_send()
    each_chunk(drain)


def local(matrix_rows, factor_bank, owner_table):
    nsec, count = lax.axis_size("sec"), lax.axis_size("col")
    sections, rows, extent = factor_bank.shape[1:]
    local_rows, columns = matrix_rows.shape
    half, chips = extent // 2, count // 2
    width = WIDTH if columns % WIDTH == 0 else columns
    chunks = columns // width
    units = ROUNDS * sections
    f32, bf16, dma = jnp.float32, jnp.bfloat16, pltpu.SemaphoreType.DMA
    return pl.pallas_call(
        functools.partial(strip_kernel, nsec, count, chunks, width),
        out_shape=pltpu.VMEM(matrix_rows.shape, matrix_rows.dtype),
        in_specs=[
            pl.BlockSpec(memory_space=pltpu.SMEM),
            pl.BlockSpec(memory_space=pl.ANY),
            pl.BlockSpec(memory_space=pl.ANY),
        ],
        out_specs=pl.BlockSpec(memory_space=pltpu.VMEM),
        scratch_shapes=[
            pltpu.VMEM((chunks, half + local_rows, width), f32),
            pltpu.VMEM((chunks, half + local_rows, width), f32),
            pltpu.VMEM((chunks, local_rows, width), f32),
            pltpu.VMEM((chunks, half, width), f32),
            pltpu.VMEM((units, extent, extent), bf16),
            pltpu.VMEM((units, extent, extent), bf16),
            *[pltpu.VMEM((2, chips, rows, extent), f32) for _ in range(units)],
            dma((sections, chunks)),
            dma((units,)),
            dma((2, chips - 1, PIECES)),
            dma((2, chips - 1, PIECES)),
            dma((2, 2 * chips - 1, PIECES)),
            dma((2, units, chips - 1)),
            dma((2, units)),
            dma((2, 4, chunks)),
        ],
        compiler_params=pltpu.CompilerParams(
            collective_id=0, has_side_effects=True, vmem_limit_bytes=50 << 20
        ),
        name="strip",
    )(owner_table, matrix_rows, factor_bank)


def solution(mesh):
    in_specs = (P("sec", "col"), P(None, "sec", "col", None), P(None, "sec", None))
    out_specs = P("sec", "col")
    return jax.shard_map(local, mesh=mesh, in_specs=in_specs, out_specs=out_specs, check_vma=False)
```

```python
import functools

import jax
import jax.numpy as jnp
from jax import lax
from jax.experimental import pallas as pl
from jax.experimental.pallas import tpu as pltpu
from jax.sharding import PartitionSpec as P

ROUNDS = 4
WIDTH = 256
PIECES = 2


def unit_order(sections):
    order = []
    for number in range(ROUNDS):
        ks = list(range(sections))
        if number % 2 == 0:
            ks = ks[::-1]
        order += [(number, k) for k in ks]
    return order


def strip_kernel(nsec, count, chunks, width, *refs):
    table_ref, x_ref, bank_ref, out_ref = refs[:4]
    xs, sa, sb, rs, ghi, glo = refs[4:10]
    sections = bank_ref.shape[1]
    order = unit_order(sections)
    units = len(order)
    held = refs[10 : 10 + units]
    (x_sems, own_sems, up_sems, down_sems, piece_sems, far_sems, relay_sems, row_sems) = refs[10 + units :]

    extent = bank_ref.shape[3]
    half = extent // 2
    rows = bank_ref.shape[2]
    local_rows = sections * extent
    chips = count // 2
    sec = lax.axis_index("sec")
    me = lax.axis_index("col")
    chip, core = me // 2, me % 2
    partner = chip * 2 + 1 - core
    after = lax.rem(sec + 1, nsec)
    before = lax.rem(sec + nsec - 1, nsec)

    def columns(c):
        return pl.ds(pl.multiple_of(c * width, width), width)

    def load(c, k):
        return pltpu.make_async_copy(
            x_ref.at[pl.ds(k * extent, extent), columns(c)],
            xs.at[c, pl.ds(half + k * extent, extent)],
            x_sems.at[k, c],
        )

    def own(u):
        number, k = order[u]
        return pltpu.make_async_copy(bank_ref.at[number, k], held[u].at[core, chip], own_sems.at[u])

    for k in range(sections - 1, -1, -1):
        lax.fori_loop(0, chunks, lambda c, _, k=k: (load(c, k).start(), 0)[1], 0)
    for u in range(units):
        own(u).start()

    barrier = pltpu.get_barrier_semaphore()

    def greet(target):
        pl.semaphore_signal(barrier, inc=1, device_id=target, device_id_type=pl.DeviceIdType.MESH)

    has_up, has_down = chip + 1 < chips, chip > 0
    greet({"sec": after})
    greet({"sec": before})
    greet({"col": partner})
    pl.when(has_up)(lambda: greet({"col": (chip + 1) * 2 + core}))
    pl.when(has_down)(lambda: greet({"col": (chip - 1) * 2 + core}))
    pl.semaphore_wait(barrier, 3 + has_up.astype(jnp.int32) + has_down.astype(jnp.int32))

    def remote(src, dst, sems, at, target):
        return pltpu.make_async_remote_copy(
            src_ref=src,
            dst_ref=dst,
            send_sem=sems.at[(0, *at)],
            recv_sem=sems.at[(1, *at)],
            device_id=target,
            device_id_type=pl.DeviceIdType.MESH,
        )

    part = rows // PIECES
    first_number, first_k = order[0]

    def piece(p):
        return pl.ds(p * part, part)

    def pass_up(src, slot, step, p):
        return remote(src, held[0].at[core, slot, piece(p)], up_sems, (step, p), {"col": (chip + 1) * 2 + core})

    def pass_down(src, slot, step, p):
        return remote(src, held[0].at[core, slot, piece(p)], down_sems, (step, p), {"col": (chip - 1) * 2 + core})

    def pass_pair(src, slot, step, p):
        return remote(src, held[0].at[core, slot, piece(p)], piece_sems, (step, p), {"col": partner})

    def own_piece(p):
        return bank_ref.at[first_number, first_k, piece(p)]

    for p in range(PIECES):
        pl.when(has_up)(lambda p=p: pass_up(own_piece(p), chip, 0, p).start())
        pl.when(has_down)(lambda p=p: pass_down(own_piece(p), chip, 0, p).start())
    for p in range(PIECES):
        pass_pair(own_piece(p), chip, 0, p).start()
    for step in range(chips - 1):
        low, high = chip - 1 - step, chip + 1 + step
        for p in range(PIECES):

            @pl.when(low >= 0)
            def _(step=step, p=p, low=low):
                src = held[0].at[core, low, piece(p)]
                pass_up(src, low, step, p).wait_recv()
                if step + 1 < chips - 1:
                    pl.when(has_up)(lambda: pass_up(src, low, step + 1, p).start())
                pass_pair(src, low, 1 + step, p).start()

            @pl.when(high < chips)
            def _(step=step, p=p, high=high):
                src = held[0].at[core, high, piece(p)]
                pass_down(src, high, step, p).wait_recv()
                if step + 1 < chips - 1:
                    pl.when(has_down)(lambda: pass_down(src, high, step + 1, p).start())
                pass_pair(src, high, chips + step, p).start()

    def far(u, d):
        number, k = order[u]
        return remote(
            bank_ref.at[number, k],
            held[u].at[core, chip],
            far_sems,
            (u, d - 1),
            {"col": lax.rem(chip + d, chips) * 2 + core},
        )

    def far_arrival(u, d):
        return remote(
            bank_ref.at[order[u]],
            held[u].at[core, lax.rem(chip + chips - d, chips)],
            far_sems,
            (u, d - 1),
            {"col": partner},
        )

    def relay(u, side):
        return remote(held[u].at[side], held[u].at[side], relay_sems, (u,), {"col": partner})

    def order_rows(u):
        number, k = order[u]
        for b in range(count):
            place = jnp.int32(0)
            for c in range(count):
                place = jnp.where(table_ref[number, k, c] == b, c, place)
            block = held[u][place % 2, place // 2]
            high = block.astype(jnp.bfloat16)
            ghi[u, b * rows : (b + 1) * rows, :] = high
            glo[u, b * rows : (b + 1) * rows, :] = (block - high.astype(jnp.float32)).astype(jnp.bfloat16)

    own(0).wait()
    for step in range(chips - 1):
        low, high = chip - 1 - step, chip + 1 + step
        for p in range(PIECES):
            pl.when(low >= 0)(
                lambda: pass_pair(held[0].at[1 - core, low, piece(p)], low, 1 + step, p).wait_recv()
            )
            pl.when(high < chips)(
                lambda: pass_pair(held[0].at[1 - core, high, piece(p)], high, chips + step, p).wait_recv()
            )
    for p in range(PIECES):
        pass_pair(held[0].at[1 - core, chip, piece(p)], chip, 0, p).wait_recv()
    order_rows(0)

    def receive(u):
        for d in range(1, chips):
            far_arrival(u, d).wait_recv()
        own(u).wait()
        relay(u, core).start()
        relay(u, 1 - core).wait_recv()
        order_rows(u)

    def split(value):
        high = value.astype(jnp.bfloat16)
        return high, (value - high.astype(jnp.float32)).astype(jnp.bfloat16)

    def product(u, begin, size, parts):
        high, low = parts
        a, b = ghi[u, begin : begin + size, :], glo[u, begin : begin + size, :]
        dot = functools.partial(jnp.dot, preferred_element_type=jnp.float32)
        return dot(a, high) + (dot(a, low) + dot(b, high))

    index = {pair: u for u, pair in enumerate(order)}
    top = half + local_rows

    def forward(c, which, buf):
        return remote(
            buf.at[c, pl.ds(top - half, half)], buf.at[c, pl.ds(0, half)], row_sems, (which, c), {"sec": after}
        )

    def back_first(c):
        return remote(rs.at[c], sb.at[c, pl.ds(local_rows - half, half)], row_sems, (1, c), {"sec": before})

    def back_last(c):
        return remote(
            sa.at[c, pl.ds(0, half)],
            out_ref.at[pl.ds(local_rows - half, half), columns(c)],
            row_sems,
            (3, c),
            {"sec": before},
        )

    def each_chunk(body):
        lax.fori_loop(0, chunks, lambda c, _: (body(c), 0)[1], 0)

    last = sections - 1

    def begin(c):
        load(c, last).wait()
        parts = split(xs[c, half + last * extent : top])
        u = index[0, last]
        sa[c, top - half : top] = product(u, half, half, parts)
        forward(c, 0, sa).start()
        sa[c, half + last * extent : top - half] = product(u, 0, half, parts)

    each_chunk(begin)
    for u in range(1, units):
        for d in range(1, chips):
            far(u, d).start()

    for k in range(last - 1, -1, -1):
        receive(index[0, k])

        def inner(c, k=k):
            load(c, k).wait()
            at = half + k * extent
            parts = split(xs[c, at : at + extent])
            sa[c, at : at + extent] = product(index[0, k], 0, extent, parts)

        each_chunk(inner)

    receive(index[1, 0])

    def straddle(c):
        forward(c, 0, sa).wait_recv()
        parts = split(sa[c, 0:extent])
        u = index[1, 0]
        rs[c] = product(u, 0, half, parts)
        back_first(c).start()
        sb[c, 0:half] = product(u, half, half, parts)

    each_chunk(straddle)
    for k in range(1, sections):
        receive(index[1, k])

        def inner(c, k=k):
            parts = split(sa[c, k * extent : (k + 1) * extent])
            sb[c, k * extent - half : (k + 1) * extent - half] = product(index[1, k], 0, extent, parts)

        each_chunk(inner)

    for k in range(last, -1, -1):
        receive(index[2, k])

    def middle(c):
        back_first(c).wait_recv()
        parts = split(sb[c, last * extent : local_rows])
        u = index[2, last]
        xs[c, top - half : top] = product(u, half, half, parts)
        forward(c, 2, xs).start()
        xs[c, half + last * extent : top - half] = product(u, 0, half, parts)
        for k in range(last):
            at = half + k * extent
            parts = split(sb[c, k * extent : (k + 1) * extent])
            xs[c, at : at + extent] = product(index[2, k], 0, extent, parts)

    each_chunk(middle)

    for k in range(sections):
        receive(index[3, k])

    def finish(c):
        forward(c, 2, xs).wait_recv()
        parts = split(xs[c, 0:extent])
        u = index[3, 0]
        sa[c, 0:half] = product(u, 0, half, parts)
        back_last(c).start()
        out_ref[0:half, columns(c)] = product(u, half, half, parts)
        for k in range(1, sections):
            parts = split(xs[c, k * extent : (k + 1) * extent])
            out_ref[k * extent - half : (k + 1) * extent - half, columns(c)] = product(
                index[3, k], 0, extent, parts
            )

    each_chunk(finish)

    def drain(c):
        forward(c, 0, sa).wait_send()
        back_first(c).wait_send()
        forward(c, 2, xs).wait_send()
        back_last(c).wait_send()
        back_last(c).wait_recv()

    for p in range(PIECES):
        pass_pair(own_piece(p), chip, 0, p).wait_send()
        pl.when(has_up)(lambda p=p: pass_up(own_piece(p), chip, 0, p).wait_send())
        pl.when(has_down)(lambda p=p: pass_down(own_piece(p), chip, 0, p).wait_send())
        for step in range(chips - 1):
            low, high = chip - 1 - step, chip + 1 + step

            @pl.when(low >= 0)
            def _():
                if step + 1 < chips - 1:
                    pl.when(has_up)(lambda: pass_up(held[0].at[core, low, piece(p)], low, step + 1, p).wait_send())
                pass_pair(held[0].at[core, low, piece(p)], low, 1 + step, p).wait_send()

            @pl.when(high < chips)
            def _():
                if step + 1 < chips - 1:
                    pl.when(has_down)(
                        lambda: pass_down(held[0].at[core, high, piece(p)], high, step + 1, p).wait_send()
                    )
                pass_pair(held[0].at[core, high, piece(p)], high, chips + step, p).wait_send()

    for u in range(1, units):
        for d in range(1, chips):
            far(u, d).wait_send()
        relay(u, core).wait_send()
    each_chunk(drain)


def local(matrix_rows, factor_bank, owner_table):
    nsec, count = lax.axis_size("sec"), lax.axis_size("col")
    sections, rows, extent = factor_bank.shape[1:]
    local_rows, columns = matrix_rows.shape
    half, chips = extent // 2, count // 2
    width = WIDTH if columns % WIDTH == 0 else columns
    chunks = columns // width
    units = ROUNDS * sections
    f32, bf16, dma = jnp.float32, jnp.bfloat16, pltpu.SemaphoreType.DMA
    return pl.pallas_call(
        functools.partial(strip_kernel, nsec, count, chunks, width),
        out_shape=pltpu.VMEM(matrix_rows.shape, matrix_rows.dtype),
        in_specs=[
            pl.BlockSpec(memory_space=pltpu.SMEM),
            pl.BlockSpec(memory_space=pl.ANY),
            pl.BlockSpec(memory_space=pl.ANY),
        ],
        out_specs=pl.BlockSpec(memory_space=pltpu.VMEM),
        scratch_shapes=[
            pltpu.VMEM((chunks, half + local_rows, width), f32),
            pltpu.VMEM((chunks, half + local_rows, width), f32),
            pltpu.VMEM((chunks, local_rows, width), f32),
            pltpu.VMEM((chunks, half, width), f32),
            pltpu.VMEM((units, extent, extent), bf16),
            pltpu.VMEM((units, extent, extent), bf16),
            *[pltpu.VMEM((2, chips, rows, extent), f32) for _ in range(units)],
            dma((sections, chunks)),
            dma((units,)),
            dma((2, chips - 1, PIECES)),
            dma((2, chips - 1, PIECES)),
            dma((2, 2 * chips - 1, PIECES)),
            dma((2, units, chips - 1)),
            dma((2, units)),
            dma((2, 4, chunks)),
        ],
        compiler_params=pltpu.CompilerParams(
            collective_id=0, has_side_effects=True, vmem_limit_bytes=50 << 20
        ),
        name="strip",
    )(owner_table, matrix_rows, factor_bank)


def solution(mesh):
    in_specs = (P("sec", "col"), P(None, "sec", "col", None), P(None, "sec", None))
    out_specs = P("sec", "col")
    return jax.shard_map(local, mesh=mesh, in_specs=in_specs, out_specs=out_specs, check_vma=False)
```

```python
import functools

import jax
import jax.numpy as jnp
from jax import lax
from jax.experimental import pallas as pl
from jax.experimental.pallas import tpu as pltpu
from jax.sharding import PartitionSpec as P

ROUNDS = 4
WIDTH = 256
PIECES = 2


def unit_order(sections):
    order = []
    for number in range(ROUNDS):
        ks = list(range(sections))
        if number % 2 == 0:
            ks = ks[::-1]
        order += [(number, k) for k in ks]
    return order


def strip_kernel(nsec, count, chunks, width, *refs):
    table_ref, x_ref, bank_ref, out_ref = refs[:4]
    xs, sa, sb, rs, ghi, glo, raw, names, named, ahi, alo = refs[4:15]
    sections = bank_ref.shape[1]
    order = unit_order(sections)
    units = len(order)
    held = refs[15 : 16 + units]
    (x_sems, own_sems, up_sems, down_sems, piece_sems, far_sems, relay_sems, row_sems, raw_sems) = refs[16 + units :]

    extent = bank_ref.shape[3]
    half = extent // 2
    rows = bank_ref.shape[2]
    local_rows = sections * extent
    chips = count // 2
    sec = lax.axis_index("sec")
    me = lax.axis_index("col")
    chip, core = me // 2, me % 2
    partner = chip * 2 + 1 - core
    after = lax.rem(sec + 1, nsec)
    before = lax.rem(sec + nsec - 1, nsec)

    def columns(c):
        return pl.ds(pl.multiple_of(c * width, width), width)

    def load(c, k):
        return pltpu.make_async_copy(
            x_ref.at[pl.ds(k * extent, extent), columns(c)],
            xs.at[c, pl.ds(half + k * extent, extent)],
            x_sems.at[k, c],
        )

    def own(u):
        number, k = order[u]
        return pltpu.make_async_copy(bank_ref.at[number, k], held[u].at[core, chip], own_sems.at[u])

    for k in range(sections - 1, -1, -1):
        lax.fori_loop(0, chunks, lambda c, _, k=k: (load(c, k).start(), 0)[1], 0)
    for u in range(units):
        own(u).start()

    barrier = pltpu.get_barrier_semaphore()

    def greet(target):
        pl.semaphore_signal(barrier, inc=1, device_id=target, device_id_type=pl.DeviceIdType.MESH)

    has_up, has_down = chip + 1 < chips, chip > 0
    greet({"sec": after})
    greet({"sec": before})
    greet({"col": partner})
    pl.when(has_up)(lambda: greet({"col": (chip + 1) * 2 + core}))
    pl.when(has_down)(lambda: greet({"col": (chip - 1) * 2 + core}))
    pl.semaphore_wait(barrier, 3 + has_up.astype(jnp.int32) + has_down.astype(jnp.int32))

    def remote(src, dst, sems, at, target):
        return pltpu.make_async_remote_copy(
            src_ref=src,
            dst_ref=dst,
            send_sem=sems.at[(0, *at)],
            recv_sem=sems.at[(1, *at)],
            device_id=target,
            device_id_type=pl.DeviceIdType.MESH,
        )

    early = chunks - 1
    last = sections - 1
    extra = units

    def raw_block():
        return remote(bank_ref.at[0, last], held[extra].at[core, chip], raw_sems, (0,), {"sec": after})

    def raw_names():
        return remote(names, named, raw_sems, (1,), {"sec": after})

    def raw_rows():
        return remote(
            x_ref.at[pl.ds(last * extent, extent), pl.ds(early * width, width)], raw, raw_sems, (2,), {"sec": after}
        )

    raw_block().start()
    raw_rows().start()

    part = rows // PIECES
    first_number, first_k = order[0]

    def piece(p):
        return pl.ds(p * part, part)

    def pass_up(src, slot, step, p):
        return remote(src, held[0].at[core, slot, piece(p)], up_sems, (step, p), {"col": (chip + 1) * 2 + core})

    def pass_down(src, slot, step, p):
        return remote(src, held[0].at[core, slot, piece(p)], down_sems, (step, p), {"col": (chip - 1) * 2 + core})

    def pass_pair(src, slot, step, p):
        return remote(src, held[0].at[core, slot, piece(p)], piece_sems, (step, p), {"col": partner})

    def own_piece(p):
        return bank_ref.at[first_number, first_k, piece(p)]

    for p in range(PIECES):
        pl.when(has_up)(lambda p=p: pass_up(own_piece(p), chip, 0, p).start())
        pl.when(has_down)(lambda p=p: pass_down(own_piece(p), chip, 0, p).start())
    for p in range(PIECES):
        pass_pair(own_piece(p), chip, 0, p).start()
    for step in range(chips - 1):
        low, high = chip - 1 - step, chip + 1 + step
        for p in range(PIECES):

            @pl.when(low >= 0)
            def _(step=step, p=p, low=low):
                src = held[0].at[core, low, piece(p)]
                pass_up(src, low, step, p).wait_recv()
                if step + 1 < chips - 1:
                    pl.when(has_up)(lambda: pass_up(src, low, step + 1, p).start())
                pass_pair(src, low, 1 + step, p).start()

            @pl.when(high < chips)
            def _(step=step, p=p, high=high):
                src = held[0].at[core, high, piece(p)]
                pass_down(src, high, step, p).wait_recv()
                if step + 1 < chips - 1:
                    pl.when(has_down)(lambda: pass_down(src, high, step + 1, p).start())
                pass_pair(src, high, chips + step, p).start()

    for p in range(count):
        names[p : p + 1, :] = jnp.full((1, extent), table_ref[0, last, p].astype(jnp.float32))
    raw_names().start()

    def far(u, d):
        return remote(
            held[extra].at[core, chip] if u == extra else bank_ref.at[order[u]],
            held[u].at[core, chip],
            far_sems,
            (u, d - 1),
            {"col": lax.rem(chip + d, chips) * 2 + core},
        )

    def far_arrival(u, d):
        return remote(
            bank_ref.at[0, 0],
            held[u].at[core, lax.rem(chip + chips - d, chips)],
            far_sems,
            (u, d - 1),
            {"col": partner},
        )

    def relay(u, side):
        return remote(held[u].at[side], held[u].at[side], relay_sems, (u,), {"col": partner})

    def order_rows(u):
        number, k = order[u]
        for b in range(count):
            place = jnp.int32(0)
            for c in range(count):
                place = jnp.where(table_ref[number, k, c] == b, c, place)
            block = held[u][place % 2, place // 2]
            high = block.astype(jnp.bfloat16)
            ghi[u, b * rows : (b + 1) * rows, :] = high
            glo[u, b * rows : (b + 1) * rows, :] = (block - high.astype(jnp.float32)).astype(jnp.bfloat16)

    own(0).wait()
    for step in range(chips - 1):
        low, high = chip - 1 - step, chip + 1 + step
        for p in range(PIECES):
            pl.when(low >= 0)(
                lambda: pass_pair(held[0].at[1 - core, low, piece(p)], low, 1 + step, p).wait_recv()
            )
            pl.when(high < chips)(
                lambda: pass_pair(held[0].at[1 - core, high, piece(p)], high, chips + step, p).wait_recv()
            )
    for p in range(PIECES):
        pass_pair(held[0].at[1 - core, chip, piece(p)], chip, 0, p).wait_recv()
    order_rows(0)

    def collect(u):
        for d in range(1, chips):
            far_arrival(u, d).wait_recv()
        if u != extra:
            own(u).wait()
        relay(u, core).start()
        relay(u, 1 - core).wait_recv()

    def receive(u):
        collect(u)
        order_rows(u)

    def split(value):
        high = value.astype(jnp.bfloat16)
        return high, (value - high.astype(jnp.float32)).astype(jnp.bfloat16)

    def product(u, begin, size, parts):
        high, low = parts
        a, b = ghi[u, begin : begin + size, :], glo[u, begin : begin + size, :]
        dot = functools.partial(jnp.dot, preferred_element_type=jnp.float32)
        return dot(a, high) + (dot(a, low) + dot(b, high))

    index = {pair: u for u, pair in enumerate(order)}
    top = half + local_rows

    def forward(c, which, buf):
        return remote(
            buf.at[c, pl.ds(top - half, half)], buf.at[c, pl.ds(0, half)], row_sems, (which, c), {"sec": after}
        )

    def back_first(c):
        return remote(rs.at[c], sb.at[c, pl.ds(local_rows - half, half)], row_sems, (1, c), {"sec": before})

    def back_last(c):
        return remote(
            sa.at[c, pl.ds(0, half)],
            out_ref.at[pl.ds(local_rows - half, half), columns(c)],
            row_sems,
            (3, c),
            {"sec": before},
        )

    def each_chunk(body, stop=chunks):
        lax.fori_loop(0, stop, lambda c, _: (body(c), 0)[1], 0)


    def begin(c):
        load(c, last).wait()
        parts = split(xs[c, half + last * extent : top])
        u = index[0, last]
        sa[c, top - half : top] = product(u, half, half, parts)
        pl.when(c != early)(lambda: forward(c, 0, sa).start())
        sa[c, half + last * extent : top - half] = product(u, 0, half, parts)

    each_chunk(begin)
    raw_block().wait_recv()
    for u in (1, 2, extra, *range(3, units)):
        for d in range(1, chips):
            far(u, d).start()

    for k in range(last - 1, -1, -1):
        receive(index[0, k])

        def inner(c, k=k):
            load(c, k).wait()
            at = half + k * extent
            parts = split(xs[c, at : at + extent])
            sa[c, at : at + extent] = product(index[0, k], 0, extent, parts)

        each_chunk(inner)

    receive(index[1, 0])

    def straddle(c):
        pl.when(c != early)(lambda: forward(c, 0, sa).wait_recv())
        parts = split(sa[c, 0:extent])
        u = index[1, 0]
        rs[c] = product(u, 0, half, parts)
        back_first(c).start()
        sb[c, 0:half] = product(u, half, half, parts)

    each_chunk(straddle, early)

    collect(extra)
    raw_names().wait_recv()
    raw_rows().wait_recv()
    for b in range(count // 2, count):
        block = jnp.zeros((rows, extent), jnp.float32)
        for p in range(count):
            number_of = jnp.broadcast_to(named[p : p + 1, :], (rows, extent))
            block = jnp.where(number_of == float(b), held[extra][p % 2, p // 2], block)
        at = (b - count // 2) * rows
        ahi[at : at + rows, :], alo[at : at + rows, :] = split(block)
    dot = functools.partial(jnp.dot, preferred_element_type=jnp.float32)
    high, low = split(raw[...])
    sa[early, 0:half] = dot(ahi[...], high) + (dot(ahi[...], low) + dot(alo[...], high))
    straddle(early)
    for k in range(1, sections):
        receive(index[1, k])

        def inner(c, k=k):
            parts = split(sa[c, k * extent : (k + 1) * extent])
            sb[c, k * extent - half : (k + 1) * extent - half] = product(index[1, k], 0, extent, parts)

        each_chunk(inner)

    for k in range(last, -1, -1):
        receive(index[2, k])

    def middle(c):
        back_first(c).wait_recv()
        parts = split(sb[c, last * extent : local_rows])
        u = index[2, last]
        xs[c, top - half : top] = product(u, half, half, parts)
        forward(c, 2, xs).start()
        xs[c, half + last * extent : top - half] = product(u, 0, half, parts)
        for k in range(last):
            at = half + k * extent
            parts = split(sb[c, k * extent : (k + 1) * extent])
            xs[c, at : at + extent] = product(index[2, k], 0, extent, parts)

    each_chunk(middle)

    for k in range(sections):
        receive(index[3, k])

    def finish(c):
        forward(c, 2, xs).wait_recv()
        parts = split(xs[c, 0:extent])
        u = index[3, 0]
        sa[c, 0:half] = product(u, 0, half, parts)
        back_last(c).start()
        out_ref[0:half, columns(c)] = product(u, half, half, parts)
        for k in range(1, sections):
            parts = split(xs[c, k * extent : (k + 1) * extent])
            out_ref[k * extent - half : (k + 1) * extent - half, columns(c)] = product(
                index[3, k], 0, extent, parts
            )

    each_chunk(finish)

    def drain(c):
        pl.when(c != early)(lambda: forward(c, 0, sa).wait_send())
        back_first(c).wait_send()
        forward(c, 2, xs).wait_send()
        back_last(c).wait_send()
        back_last(c).wait_recv()

    for p in range(PIECES):
        pass_pair(own_piece(p), chip, 0, p).wait_send()
        pl.when(has_up)(lambda p=p: pass_up(own_piece(p), chip, 0, p).wait_send())
        pl.when(has_down)(lambda p=p: pass_down(own_piece(p), chip, 0, p).wait_send())
        for step in range(chips - 1):
            low, high = chip - 1 - step, chip + 1 + step

            @pl.when(low >= 0)
            def _():
                if step + 1 < chips - 1:
                    pl.when(has_up)(lambda: pass_up(held[0].at[core, low, piece(p)], low, step + 1, p).wait_send())
                pass_pair(held[0].at[core, low, piece(p)], low, 1 + step, p).wait_send()

            @pl.when(high < chips)
            def _():
                if step + 1 < chips - 1:
                    pl.when(has_down)(
                        lambda: pass_down(held[0].at[core, high, piece(p)], high, step + 1, p).wait_send()
                    )
                pass_pair(held[0].at[core, high, piece(p)], high, chips + step, p).wait_send()

    for u in range(1, units + 1):
        for d in range(1, chips):
            far(u, d).wait_send()
        relay(u, core).wait_send()
    raw_block().wait_send()
    raw_names().wait_send()
    raw_rows().wait_send()
    each_chunk(drain)


def local(matrix_rows, factor_bank, owner_table):
    nsec, count = lax.axis_size("sec"), lax.axis_size("col")
    sections, rows, extent = factor_bank.shape[1:]
    local_rows, columns = matrix_rows.shape
    half, chips = extent // 2, count // 2
    width = WIDTH if columns % WIDTH == 0 else columns
    chunks = columns // width
    units = ROUNDS * sections
    f32, bf16, dma = jnp.float32, jnp.bfloat16, pltpu.SemaphoreType.DMA
    return pl.pallas_call(
        functools.partial(strip_kernel, nsec, count, chunks, width),
        out_shape=pltpu.VMEM(matrix_rows.shape, matrix_rows.dtype),
        in_specs=[
            pl.BlockSpec(memory_space=pltpu.SMEM),
            pl.BlockSpec(memory_space=pl.ANY),
            pl.BlockSpec(memory_space=pl.ANY),
        ],
        out_specs=pl.BlockSpec(memory_space=pltpu.VMEM),
        scratch_shapes=[
            pltpu.VMEM((chunks, half + local_rows, width), f32),
            pltpu.VMEM((chunks, half + local_rows, width), f32),
            pltpu.VMEM((chunks, local_rows, width), f32),
            pltpu.VMEM((chunks, half, width), f32),
            pltpu.VMEM((units, extent, extent), bf16),
            pltpu.VMEM((units, extent, extent), bf16),
            pltpu.VMEM((extent, width), f32),
            pltpu.VMEM((count, extent), f32),
            pltpu.VMEM((count, extent), f32),
            pltpu.VMEM((half, extent), bf16),
            pltpu.VMEM((half, extent), bf16),
            *[pltpu.VMEM((2, chips, rows, extent), f32) for _ in range(units + 1)],
            dma((sections, chunks)),
            dma((units,)),
            dma((2, chips - 1, PIECES)),
            dma((2, chips - 1, PIECES)),
            dma((2, 2 * chips - 1, PIECES)),
            dma((2, units + 1, chips - 1)),
            dma((2, units + 1)),
            dma((2, 4, chunks)),
            dma((2, 3)),
        ],
        compiler_params=pltpu.CompilerParams(
            collective_id=0, has_side_effects=True, vmem_limit_bytes=54 << 20
        ),
        name="strip",
    )(owner_table, matrix_rows, factor_bank)


def solution(mesh):
    in_specs = (P("sec", "col"), P(None, "sec", "col", None), P(None, "sec", None))
    out_specs = P("sec", "col")
    return jax.shard_map(local, mesh=mesh, in_specs=in_specs, out_specs=out_specs, check_vma=False)
```

```python
import functools

import jax
import jax.numpy as jnp
from jax import lax
from jax.experimental import pallas as pl
from jax.experimental.pallas import tpu as pltpu
from jax.sharding import PartitionSpec as P

ROUNDS = 4
WIDTH = 256
PIECES = 2
AHEAD = 3


def unit_order(sections):
    order = []
    for number in range(ROUNDS):
        ks = list(range(sections))
        if number % 2 == 0:
            ks = ks[::-1]
        order += [(number, k) for k in ks]
    return order


def strip_kernel(nsec, count, chunks, width, *refs):
    owners_ref, x_ref, bank_ref, out_ref = refs[:4]
    xs, sa, sb, rs, ghi, glo, raw, names, named, ahi, alo, table_ref = refs[4:16]
    sections = bank_ref.shape[1]
    order = unit_order(sections)
    units = len(order)
    held = refs[16 : 17 + units]
    (x_sems, own_sems, up_sems, down_sems, piece_sems, far_sems, relay_sems, row_sems, raw_sems, table_sem) = refs[17 + units :]

    extent = bank_ref.shape[3]
    half = extent // 2
    rows = bank_ref.shape[2]
    local_rows = sections * extent
    chips = count // 2
    sec = lax.axis_index("sec")
    me = lax.axis_index("col")
    chip, core = me // 2, me % 2
    partner = chip * 2 + 1 - core
    after = lax.rem(sec + 1, nsec)
    before = lax.rem(sec + nsec - 1, nsec)

    def columns(c):
        return pl.ds(pl.multiple_of(c * width, width), width)

    def load(c, k):
        return pltpu.make_async_copy(
            x_ref.at[pl.ds(k * extent, extent), columns(c)],
            xs.at[c, pl.ds(half + k * extent, extent)],
            x_sems.at[k, c],
        )

    def own(u):
        number, k = order[u]
        return pltpu.make_async_copy(bank_ref.at[number, k], held[u].at[core, chip], own_sems.at[u])

    barrier = pltpu.get_barrier_semaphore()

    def greet(target):
        pl.semaphore_signal(barrier, inc=1, device_id=target, device_id_type=pl.DeviceIdType.MESH)

    has_up, has_down = chip + 1 < chips, chip > 0
    greet({"sec": after})
    greet({"sec": before})
    greet({"col": partner})
    pl.when(has_up)(lambda: greet({"col": (chip + 1) * 2 + core}))
    pl.when(has_down)(lambda: greet({"col": (chip - 1) * 2 + core}))
    table = pltpu.make_async_copy(owners_ref, table_ref, table_sem)
    table.start()
    for k in range(sections - 1, -1, -1):
        lax.fori_loop(0, chunks, lambda c, _, k=k: (load(c, k).start(), 0)[1], 0)
    for u in range(units):
        own(u).start()
    pl.semaphore_wait(barrier, 3 + has_up.astype(jnp.int32) + has_down.astype(jnp.int32))

    def remote(src, dst, sems, at, target):
        return pltpu.make_async_remote_copy(
            src_ref=src,
            dst_ref=dst,
            send_sem=sems.at[(0, *at)],
            recv_sem=sems.at[(1, *at)],
            device_id=target,
            device_id_type=pl.DeviceIdType.MESH,
        )

    early = chunks - 1
    last = sections - 1
    extra = units

    def raw_block():
        return remote(bank_ref.at[0, last], held[extra].at[core, chip], raw_sems, (0,), {"sec": after})

    def raw_names():
        return remote(names, named, raw_sems, (1,), {"sec": after})

    def raw_rows():
        return remote(
            x_ref.at[pl.ds(last * extent, extent), pl.ds(early * width, width)], raw, raw_sems, (2,), {"sec": after}
        )

    raw_block().start()
    raw_rows().start()

    part = rows // PIECES
    first_number, first_k = order[0]

    def piece(p):
        return pl.ds(p * part, part)

    def pass_up(src, slot, step, p):
        return remote(src, held[0].at[core, slot, piece(p)], up_sems, (step, p), {"col": (chip + 1) * 2 + core})

    def pass_down(src, slot, step, p):
        return remote(src, held[0].at[core, slot, piece(p)], down_sems, (step, p), {"col": (chip - 1) * 2 + core})

    def pass_pair(src, slot, step, p):
        return remote(src, held[0].at[core, slot, piece(p)], piece_sems, (step, p), {"col": partner})

    def own_piece(p):
        return bank_ref.at[first_number, first_k, piece(p)]

    for p in range(PIECES):
        pl.when(has_up)(lambda p=p: pass_up(own_piece(p), chip, 0, p).start())
        pl.when(has_down)(lambda p=p: pass_down(own_piece(p), chip, 0, p).start())
    for p in range(PIECES):
        pass_pair(own_piece(p), chip, 0, p).start()
    for step in range(chips - 1):
        low, high = chip - 1 - step, chip + 1 + step
        for p in range(PIECES):

            @pl.when(low >= 0)
            def _(step=step, p=p, low=low):
                src = held[0].at[core, low, piece(p)]
                pass_up(src, low, step, p).wait_recv()
                if step + 1 < chips - 1:
                    pl.when(has_up)(lambda: pass_up(src, low, step + 1, p).start())
                pass_pair(src, low, 1 + step, p).start()

            @pl.when(high < chips)
            def _(step=step, p=p, high=high):
                src = held[0].at[core, high, piece(p)]
                pass_down(src, high, step, p).wait_recv()
                if step + 1 < chips - 1:
                    pl.when(has_down)(lambda: pass_down(src, high, step + 1, p).start())
                pass_pair(src, high, chips + step, p).start()

    table.wait()
    for p in range(count):
        names[p : p + 1, :] = jnp.full((1, extent), table_ref[0, last, p].astype(jnp.float32))
    raw_names().start()

    def far(u, d):
        return remote(
            held[extra].at[core, chip] if u == extra else bank_ref.at[order[u]],
            held[u].at[core, chip],
            far_sems,
            (u, d - 1),
            {"col": lax.rem(chip + d, chips) * 2 + core},
        )

    def far_arrival(u, d):
        return remote(
            bank_ref.at[0, 0],
            held[u].at[core, lax.rem(chip + chips - d, chips)],
            far_sems,
            (u, d - 1),
            {"col": partner},
        )

    def relay(u, side):
        return remote(held[u].at[side], held[u].at[side], relay_sems, (u,), {"col": partner})

    def order_rows(u):
        number, k = order[u]
        for b in range(count):
            place = jnp.int32(0)
            for c in range(count):
                place = jnp.where(table_ref[number, k, c] == b, c, place)
            block = held[u][place % 2, place // 2]
            high = block.astype(jnp.bfloat16)
            ghi[u, b * rows : (b + 1) * rows, :] = high
            glo[u, b * rows : (b + 1) * rows, :] = (block - high.astype(jnp.float32)).astype(jnp.bfloat16)

    own(0).wait()
    for step in range(chips - 1):
        low, high = chip - 1 - step, chip + 1 + step
        for p in range(PIECES):
            pl.when(low >= 0)(
                lambda: pass_pair(held[0].at[1 - core, low, piece(p)], low, 1 + step, p).wait_recv()
            )
            pl.when(high < chips)(
                lambda: pass_pair(held[0].at[1 - core, high, piece(p)], high, chips + step, p).wait_recv()
            )
    for p in range(PIECES):
        pass_pair(held[0].at[1 - core, chip, piece(p)], chip, 0, p).wait_recv()
    order_rows(0)

    def collect(u):
        for d in range(1, chips):
            far_arrival(u, d).wait_recv()
        if u != extra:
            own(u).wait()
        relay(u, core).start()
        relay(u, 1 - core).wait_recv()

    def receive(u):
        collect(u)
        order_rows(u)

    def split(value):
        high = value.astype(jnp.bfloat16)
        return high, (value - high.astype(jnp.float32)).astype(jnp.bfloat16)

    def product(u, begin, size, parts):
        high, low = parts
        a, b = ghi[u, begin : begin + size, :], glo[u, begin : begin + size, :]
        dot = functools.partial(jnp.dot, preferred_element_type=jnp.float32)
        return dot(a, high) + (dot(a, low) + dot(b, high))

    index = {pair: u for u, pair in enumerate(order)}
    top = half + local_rows

    def forward(c, which, buf):
        return remote(
            buf.at[c, pl.ds(top - half, half)], buf.at[c, pl.ds(0, half)], row_sems, (which, c), {"sec": after}
        )

    def back_first(c):
        return remote(rs.at[c], sb.at[c, pl.ds(local_rows - half, half)], row_sems, (1, c), {"sec": before})

    def back_last(c):
        return remote(
            sa.at[c, pl.ds(0, half)],
            out_ref.at[pl.ds(local_rows - half, half), columns(c)],
            row_sems,
            (3, c),
            {"sec": before},
        )

    def each_chunk(body, start=0, stop=chunks):
        lax.fori_loop(start, stop, lambda c, _: (body(c), 0)[1], 0)


    def begin(c):
        load(c, last).wait()
        parts = split(xs[c, half + last * extent : top])
        u = index[0, last]
        sa[c, top - half : top] = product(u, half, half, parts)
        pl.when(c != early)(lambda: forward(c, 0, sa).start())
        sa[c, half + last * extent : top - half] = product(u, 0, half, parts)

    def send_far(*chosen):
        for u in chosen:
            for d in range(1, chips):
                far(u, d).start()

    each_chunk(begin, 0, AHEAD)
    send_far(1, 2)
    each_chunk(begin, AHEAD)
    raw_block().wait_recv()
    send_far(extra, *range(3, units))

    for k in range(last - 1, -1, -1):
        receive(index[0, k])

        def inner(c, k=k):
            load(c, k).wait()
            at = half + k * extent
            parts = split(xs[c, at : at + extent])
            sa[c, at : at + extent] = product(index[0, k], 0, extent, parts)

        each_chunk(inner)

    receive(index[1, 0])

    def straddle(c):
        pl.when(c != early)(lambda: forward(c, 0, sa).wait_recv())
        parts = split(sa[c, 0:extent])
        u = index[1, 0]
        rs[c] = product(u, 0, half, parts)
        back_first(c).start()
        sb[c, 0:half] = product(u, half, half, parts)

    each_chunk(straddle, stop=early)

    collect(extra)
    raw_names().wait_recv()
    raw_rows().wait_recv()
    for b in range(count // 2, count):
        block = jnp.zeros((rows, extent), jnp.float32)
        for p in range(count):
            number_of = jnp.broadcast_to(named[p : p + 1, :], (rows, extent))
            block = jnp.where(number_of == float(b), held[extra][p % 2, p // 2], block)
        at = (b - count // 2) * rows
        ahi[at : at + rows, :], alo[at : at + rows, :] = split(block)
    dot = functools.partial(jnp.dot, preferred_element_type=jnp.float32)
    high, low = split(raw[...])
    sa[early, 0:half] = dot(ahi[...], high) + (dot(ahi[...], low) + dot(alo[...], high))
    straddle(early)
    for k in range(1, sections):
        receive(index[1, k])

        def inner(c, k=k):
            parts = split(sa[c, k * extent : (k + 1) * extent])
            sb[c, k * extent - half : (k + 1) * extent - half] = product(index[1, k], 0, extent, parts)

        each_chunk(inner)

    for k in range(last, -1, -1):
        receive(index[2, k])

    def middle(c):
        back_first(c).wait_recv()
        parts = split(sb[c, last * extent : local_rows])
        u = index[2, last]
        xs[c, top - half : top] = product(u, half, half, parts)
        forward(c, 2, xs).start()
        xs[c, half + last * extent : top - half] = product(u, 0, half, parts)
        for k in range(last):
            at = half + k * extent
            parts = split(sb[c, k * extent : (k + 1) * extent])
            xs[c, at : at + extent] = product(index[2, k], 0, extent, parts)

    each_chunk(middle)

    for k in range(sections):
        receive(index[3, k])

    def finish(c):
        forward(c, 2, xs).wait_recv()
        parts = split(xs[c, 0:extent])
        u = index[3, 0]
        sa[c, 0:half] = product(u, 0, half, parts)
        back_last(c).start()
        out_ref[0:half, columns(c)] = product(u, half, half, parts)
        for k in range(1, sections):
            parts = split(xs[c, k * extent : (k + 1) * extent])
            out_ref[k * extent - half : (k + 1) * extent - half, columns(c)] = product(
                index[3, k], 0, extent, parts
            )

    each_chunk(finish)

    def drain(c):
        pl.when(c != early)(lambda: forward(c, 0, sa).wait_send())
        back_first(c).wait_send()
        forward(c, 2, xs).wait_send()
        back_last(c).wait_send()
        back_last(c).wait_recv()

    for p in range(PIECES):
        pass_pair(own_piece(p), chip, 0, p).wait_send()
        pl.when(has_up)(lambda p=p: pass_up(own_piece(p), chip, 0, p).wait_send())
        pl.when(has_down)(lambda p=p: pass_down(own_piece(p), chip, 0, p).wait_send())
        for step in range(chips - 1):
            low, high = chip - 1 - step, chip + 1 + step

            @pl.when(low >= 0)
            def _():
                if step + 1 < chips - 1:
                    pl.when(has_up)(lambda: pass_up(held[0].at[core, low, piece(p)], low, step + 1, p).wait_send())
                pass_pair(held[0].at[core, low, piece(p)], low, 1 + step, p).wait_send()

            @pl.when(high < chips)
            def _():
                if step + 1 < chips - 1:
                    pl.when(has_down)(
                        lambda: pass_down(held[0].at[core, high, piece(p)], high, step + 1, p).wait_send()
                    )
                pass_pair(held[0].at[core, high, piece(p)], high, chips + step, p).wait_send()

    for u in range(1, units + 1):
        for d in range(1, chips):
            far(u, d).wait_send()
        relay(u, core).wait_send()
    raw_block().wait_send()
    raw_names().wait_send()
    raw_rows().wait_send()
    each_chunk(drain)


def local(matrix_rows, factor_bank, owner_table):
    nsec, count = lax.axis_size("sec"), lax.axis_size("col")
    sections, rows, extent = factor_bank.shape[1:]
    local_rows, columns = matrix_rows.shape
    half, chips = extent // 2, count // 2
    width = WIDTH if columns % WIDTH == 0 else columns
    chunks = columns // width
    units = ROUNDS * sections
    f32, bf16, dma = jnp.float32, jnp.bfloat16, pltpu.SemaphoreType.DMA
    return pl.pallas_call(
        functools.partial(strip_kernel, nsec, count, chunks, width),
        out_shape=pltpu.VMEM(matrix_rows.shape, matrix_rows.dtype),
        in_specs=[
            pl.BlockSpec(memory_space=pl.ANY),
            pl.BlockSpec(memory_space=pl.ANY),
            pl.BlockSpec(memory_space=pl.ANY),
        ],
        out_specs=pl.BlockSpec(memory_space=pltpu.VMEM),
        scratch_shapes=[
            pltpu.VMEM((chunks, half + local_rows, width), f32),
            pltpu.VMEM((chunks, half + local_rows, width), f32),
            pltpu.VMEM((chunks, local_rows, width), f32),
            pltpu.VMEM((chunks, half, width), f32),
            pltpu.VMEM((units, extent, extent), bf16),
            pltpu.VMEM((units, extent, extent), bf16),
            pltpu.VMEM((extent, width), f32),
            pltpu.VMEM((count, extent), f32),
            pltpu.VMEM((count, extent), f32),
            pltpu.VMEM((half, extent), bf16),
            pltpu.VMEM((half, extent), bf16),
            pltpu.SMEM((ROUNDS, sections, count), jnp.int32),
            *[pltpu.VMEM((2, chips, rows, extent), f32) for _ in range(units + 1)],
            dma((sections, chunks)),
            dma((units,)),
            dma((2, chips - 1, PIECES)),
            dma((2, chips - 1, PIECES)),
            dma((2, 2 * chips - 1, PIECES)),
            dma((2, units + 1, chips - 1)),
            dma((2, units + 1)),
            dma((2, 4, chunks)),
            dma((2, 3)),
            dma(()),
        ],
        compiler_params=pltpu.CompilerParams(
            collective_id=0, has_side_effects=True, vmem_limit_bytes=54 << 20
        ),
        name="strip",
    )(owner_table, matrix_rows, factor_bank)


def solution(mesh):
    in_specs = (P("sec", "col"), P(None, "sec", "col", None), P(None, "sec", None))
    out_specs = P("sec", "col")
    return jax.shard_map(local, mesh=mesh, in_specs=in_specs, out_specs=out_specs, check_vma=False)
```

```python
import functools

import jax
import jax.numpy as jnp
from jax import lax
from jax.experimental import pallas as pl
from jax.experimental.pallas import tpu as pltpu
from jax.sharding import PartitionSpec as P

ROUNDS = 4
WIDTH = 256
PIECES = 2
AHEAD = 3


def unit_order(sections):
    order = []
    for number in range(ROUNDS):
        ks = list(range(sections))
        if number % 2 == 0:
            ks = ks[::-1]
        order += [(number, k) for k in ks]
    return order


def strip_kernel(nsec, count, chunks, width, *refs):
    owners_ref, x_ref, bank_ref, out_ref = refs[:4]
    xs, sa, sb, rs, ghi, glo, raw, names, named, ahi, alo, table_ref = refs[4:16]
    sections = bank_ref.shape[1]
    order = unit_order(sections)
    units = len(order)
    held = refs[16 : 17 + units]
    (x_sems, own_sem, line_sends, line_sems, pair_sem, far_send, far_sems, relay_send, relay_sems) = refs[17 + units : 26 + units]
    (row_sends, row_sems, return_sem, raw_sends, raw_sems, table_sem) = refs[26 + units :]

    extent = bank_ref.shape[3]
    half = extent // 2
    rows = bank_ref.shape[2]
    local_rows = sections * extent
    chips = count // 2
    sec = lax.axis_index("sec")
    me = lax.axis_index("col")
    chip, core = me // 2, me % 2
    partner = chip * 2 + 1 - core
    after = lax.rem(sec + 1, nsec)
    before = lax.rem(sec + nsec - 1, nsec)

    def columns(c):
        return pl.ds(pl.multiple_of(c * width, width), width)

    def load(c, k):
        return pltpu.make_async_copy(
            x_ref.at[pl.ds(k * extent, extent), columns(c)],
            xs.at[c, pl.ds(half + k * extent, extent)],
            x_sems.at[k],
        )

    def own(u):
        number, k = order[u]
        return pltpu.make_async_copy(bank_ref.at[number, k], held[u].at[core, chip], own_sem)

    barrier = pltpu.get_barrier_semaphore()

    def greet(target):
        pl.semaphore_signal(barrier, inc=1, device_id=target, device_id_type=pl.DeviceIdType.MESH)

    has_up, has_down = chip + 1 < chips, chip > 0
    greet({"sec": after})
    greet({"sec": before})
    greet({"col": partner})
    pl.when(has_up)(lambda: greet({"col": (chip + 1) * 2 + core}))
    pl.when(has_down)(lambda: greet({"col": (chip - 1) * 2 + core}))
    table = pltpu.make_async_copy(owners_ref, table_ref, table_sem)
    table.start()
    for k in range(sections - 1, -1, -1):
        lax.fori_loop(0, chunks, lambda c, _, k=k: (load(c, k).start(), 0)[1], 0)
    for u in range(units):
        own(u).start()
    pl.semaphore_wait(barrier, 3 + has_up.astype(jnp.int32) + has_down.astype(jnp.int32))

    def settle(ref, sem):
        pltpu.make_async_copy(ref, ref, sem).wait()

    def settle_blocks(blocks, sem):
        settle(sb.at[:, pl.ds(0, blocks * rows * extent // (chunks * width))], sem)

    def remote(src, dst, send_sem, recv_sem, target):
        return pltpu.make_async_remote_copy(
            src_ref=src,
            dst_ref=dst,
            send_sem=send_sem,
            recv_sem=recv_sem,
            device_id=target,
            device_id_type=pl.DeviceIdType.MESH,
        )

    early = chunks - 1
    last = sections - 1
    extra = units

    def raw_block():
        return remote(bank_ref.at[0, last], held[extra].at[core, chip], raw_sends.at[0], raw_sems.at[0], {"sec": after})

    def raw_names():
        return remote(names, named, raw_sends.at[1], raw_sems.at[1], {"sec": after})

    def raw_rows():
        return remote(
            x_ref.at[pl.ds(last * extent, extent), pl.ds(early * width, width)],
            raw,
            raw_sends.at[2],
            raw_sems.at[2],
            {"sec": after},
        )

    raw_block().start()
    raw_rows().start()

    part = rows // PIECES
    first_number, first_k = order[0]

    def piece(p):
        return pl.ds(p * part, part)

    def passed(src, slot, p, way, target):
        return remote(src, held[0].at[core, slot, piece(p)], line_sends.at[way], line_sems.at[slot, p], {"col": target})

    def pass_up(src, slot, p):
        return passed(src, slot, p, 0, (chip + 1) * 2 + core)

    def pass_down(src, slot, p):
        return passed(src, slot, p, 1, (chip - 1) * 2 + core)

    def pass_pair(src, slot, p):
        return remote(src, held[0].at[core, slot, piece(p)], line_sends.at[2], pair_sem, {"col": partner})

    def own_piece(p):
        return bank_ref.at[first_number, first_k, piece(p)]

    for p in range(PIECES):
        pl.when(has_up)(lambda p=p: pass_up(own_piece(p), chip, p).start())
        pl.when(has_down)(lambda p=p: pass_down(own_piece(p), chip, p).start())
    for p in range(PIECES):
        pass_pair(own_piece(p), chip, p).start()
    for step in range(chips - 1):
        low, high = chip - 1 - step, chip + 1 + step
        for p in range(PIECES):

            @pl.when(low >= 0)
            def _(step=step, p=p, low=low):
                src = held[0].at[core, low, piece(p)]
                pass_up(src, low, p).wait_recv()
                if step + 1 < chips - 1:
                    pl.when(has_up)(lambda: pass_up(src, low, p).start())
                pass_pair(src, low, p).start()

            @pl.when(high < chips)
            def _(step=step, p=p, high=high):
                src = held[0].at[core, high, piece(p)]
                pass_down(src, high, p).wait_recv()
                if step + 1 < chips - 1:
                    pl.when(has_down)(lambda: pass_down(src, high, p).start())
                pass_pair(src, high, p).start()

    table.wait()
    for p in range(count):
        names[p : p + 1, :] = jnp.full((1, extent), table_ref[0, last, p].astype(jnp.float32))
    raw_names().start()

    def far(u, d):
        return remote(
            held[extra].at[core, chip] if u == extra else bank_ref.at[order[u]],
            held[u].at[core, chip],
            far_send,
            far_sems.at[u - 1],
            {"col": lax.rem(chip + d, chips) * 2 + core},
        )

    turns = []

    def relay(u, side):
        at = turns.index(u) % 2
        return remote(held[u].at[side], held[u].at[side], relay_send, relay_sems.at[at], {"col": partner})

    def order_rows(u):
        number, k = order[u]
        for b in range(count):
            place = jnp.int32(0)
            for c in range(count):
                place = jnp.where(table_ref[number, k, c] == b, c, place)
            block = held[u][place % 2, place // 2]
            high = block.astype(jnp.bfloat16)
            ghi[u, b * rows : (b + 1) * rows, :] = high
            glo[u, b * rows : (b + 1) * rows, :] = (block - high.astype(jnp.float32)).astype(jnp.bfloat16)

    settle(bank_ref, own_sem)
    settle(held[0].at[1 - core], pair_sem)
    order_rows(0)

    def collect(u):
        turns.append(u)
        settle(held[u].at[core, pl.ds(0, chips - 1)], far_sems.at[u - 1])
        relay(u, core).start()
        relay(u, 1 - core).wait_recv()

    def receive(u):
        collect(u)
        order_rows(u)

    def split(value):
        high = value.astype(jnp.bfloat16)
        return high, (value - high.astype(jnp.float32)).astype(jnp.bfloat16)

    def product(u, begin, size, parts):
        high, low = parts
        a, b = ghi[u, begin : begin + size, :], glo[u, begin : begin + size, :]
        dot = functools.partial(jnp.dot, preferred_element_type=jnp.float32)
        return dot(a, high) + (dot(a, low) + dot(b, high))

    index = {pair: u for u, pair in enumerate(order)}
    top = half + local_rows

    def forward(c, which, buf):
        return remote(
            buf.at[c, pl.ds(top - half, half)],
            buf.at[c, pl.ds(0, half)],
            row_sends.at[which],
            row_sems.at[0, c],
            {"sec": after},
        )

    def back_first(c):
        return remote(
            rs.at[c],
            sb.at[c, pl.ds(local_rows - half, half)],
            row_sends.at[1],
            row_sems.at[1, c],
            {"sec": before},
        )

    def back_last(c):
        return remote(
            sa.at[c, pl.ds(0, half)],
            out_ref.at[pl.ds(local_rows - half, half), columns(c)],
            row_sends.at[3],
            return_sem,
            {"sec": before},
        )

    def each_chunk(body, start=0, stop=chunks):
        lax.fori_loop(start, stop, lambda c, _: (body(c), 0)[1], 0)


    settle(xs.at[:, pl.ds(half + last * extent, extent)], x_sems.at[last])

    def begin(c):
        parts = split(xs[c, half + last * extent : top])
        u = index[0, last]
        sa[c, top - half : top] = product(u, half, half, parts)
        pl.when(c != early)(lambda: forward(c, 0, sa).start())
        sa[c, half + last * extent : top - half] = product(u, 0, half, parts)

    def send_far(*chosen):
        for u in chosen:
            for d in range(1, chips):
                far(u, d).start()

    each_chunk(begin, 0, AHEAD)
    send_far(1, 2)
    each_chunk(begin, AHEAD)
    raw_block().wait_recv()
    send_far(extra, *range(3, units))

    for k in range(last - 1, -1, -1):
        receive(index[0, k])
        settle(xs.at[:, pl.ds(half + k * extent, extent)], x_sems.at[k])

        def inner(c, k=k):
            at = half + k * extent
            parts = split(xs[c, at : at + extent])
            sa[c, at : at + extent] = product(index[0, k], 0, extent, parts)

        each_chunk(inner)

    receive(index[1, 0])

    def straddle(c):
        pl.when(c != early)(lambda: forward(c, 0, sa).wait_recv())
        parts = split(sa[c, 0:extent])
        u = index[1, 0]
        rs[c] = product(u, 0, half, parts)
        back_first(c).start()
        sb[c, 0:half] = product(u, half, half, parts)

    each_chunk(straddle, stop=early)

    collect(extra)
    raw_names().wait_recv()
    raw_rows().wait_recv()
    for b in range(count // 2, count):
        block = jnp.zeros((rows, extent), jnp.float32)
        for p in range(count):
            number_of = jnp.broadcast_to(named[p : p + 1, :], (rows, extent))
            block = jnp.where(number_of == float(b), held[extra][p % 2, p // 2], block)
        at = (b - count // 2) * rows
        ahi[at : at + rows, :], alo[at : at + rows, :] = split(block)
    dot = functools.partial(jnp.dot, preferred_element_type=jnp.float32)
    high, low = split(raw[...])
    sa[early, 0:half] = dot(ahi[...], high) + (dot(ahi[...], low) + dot(alo[...], high))
    straddle(early)
    for k in range(1, sections):
        receive(index[1, k])

        def inner(c, k=k):
            parts = split(sa[c, k * extent : (k + 1) * extent])
            sb[c, k * extent - half : (k + 1) * extent - half] = product(index[1, k], 0, extent, parts)

        each_chunk(inner)

    for k in range(last, -1, -1):
        receive(index[2, k])

    def middle(c):
        back_first(c).wait_recv()
        parts = split(sb[c, last * extent : local_rows])
        u = index[2, last]
        xs[c, top - half : top] = product(u, half, half, parts)
        forward(c, 2, xs).start()
        xs[c, half + last * extent : top - half] = product(u, 0, half, parts)
        for k in range(last):
            at = half + k * extent
            parts = split(sb[c, k * extent : (k + 1) * extent])
            xs[c, at : at + extent] = product(index[2, k], 0, extent, parts)

    each_chunk(middle)

    for k in range(sections):
        receive(index[3, k])

    def finish(c):
        forward(c, 2, xs).wait_recv()
        parts = split(xs[c, 0:extent])
        u = index[3, 0]
        sa[c, 0:half] = product(u, 0, half, parts)
        back_last(c).start()
        out_ref[0:half, columns(c)] = product(u, half, half, parts)
        for k in range(1, sections):
            parts = split(xs[c, k * extent : (k + 1) * extent])
            out_ref[k * extent - half : (k + 1) * extent - half, columns(c)] = product(
                index[3, k], 0, extent, parts
            )

    each_chunk(finish)

    for v in range(chips):
        if v + 1 < chips:
            pl.when(chip == v)(lambda: settle(held[0].at[core, pl.ds(0, v + 1)], line_sends.at[0]))
        if v > 0:
            pl.when(chip == v)(lambda: settle(held[0].at[core, pl.ds(0, chips - v)], line_sends.at[1]))
    settle(held[0].at[core], line_sends.at[2])
    settle_blocks(units * (chips - 1), far_send)
    settle_blocks(units * chips, relay_send)
    raw_block().wait_send()
    raw_names().wait_send()
    raw_rows().wait_send()
    if early:
        settle(sa.at[pl.ds(0, early), pl.ds(top - half, half)], row_sends.at[0])
    settle(rs, row_sends.at[1])
    settle(xs.at[:, pl.ds(top - half, half)], row_sends.at[2])
    settle(sa.at[:, pl.ds(0, half)], row_sends.at[3])
    settle(out_ref.at[pl.ds(local_rows - half, half)], return_sem)


def local(matrix_rows, factor_bank, owner_table):
    nsec, count = lax.axis_size("sec"), lax.axis_size("col")
    sections, rows, extent = factor_bank.shape[1:]
    local_rows, columns = matrix_rows.shape
    half, chips = extent // 2, count // 2
    width = WIDTH if columns % WIDTH == 0 else columns
    chunks = columns // width
    units = ROUNDS * sections
    f32, bf16, dma = jnp.float32, jnp.bfloat16, pltpu.SemaphoreType.DMA
    return pl.pallas_call(
        functools.partial(strip_kernel, nsec, count, chunks, width),
        out_shape=pltpu.VMEM(matrix_rows.shape, matrix_rows.dtype),
        in_specs=[
            pl.BlockSpec(memory_space=pl.ANY),
            pl.BlockSpec(memory_space=pl.ANY),
            pl.BlockSpec(memory_space=pl.ANY),
        ],
        out_specs=pl.BlockSpec(memory_space=pltpu.VMEM),
        scratch_shapes=[
            pltpu.VMEM((chunks, half + local_rows, width), f32),
            pltpu.VMEM((chunks, half + local_rows, width), f32),
            pltpu.VMEM((chunks, local_rows, width), f32),
            pltpu.VMEM((chunks, half, width), f32),
            pltpu.VMEM((units, extent, extent), bf16),
            pltpu.VMEM((units, extent, extent), bf16),
            pltpu.VMEM((extent, width), f32),
            pltpu.VMEM((count, extent), f32),
            pltpu.VMEM((count, extent), f32),
            pltpu.VMEM((half, extent), bf16),
            pltpu.VMEM((half, extent), bf16),
            pltpu.SMEM((ROUNDS, sections, count), jnp.int32),
            *[pltpu.VMEM((2, chips, rows, extent), f32) for _ in range(units + 1)],
            dma((sections,)),
            dma(()),
            dma((3,)),
            dma((chips, PIECES)),
            dma(()),
            dma(()),
            dma((units,)),
            dma(()),
            dma((2,)),
            dma((4,)),
            dma((2, chunks)),
            dma(()),
            dma((3,)),
            dma((3,)),
            dma(()),
        ],
        compiler_params=pltpu.CompilerParams(
            collective_id=0, has_side_effects=True, vmem_limit_bytes=54 << 20
        ),
        name="strip",
    )(owner_table, matrix_rows, factor_bank)


def solution(mesh):
    in_specs = (P("sec", "col"), P(None, "sec", "col", None), P(None, "sec", None))
    out_specs = P("sec", "col")
    return jax.shard_map(local, mesh=mesh, in_specs=in_specs, out_specs=out_specs, check_vma=False)
```

```python
import functools

import jax
import jax.numpy as jnp
from jax import lax
from jax.experimental import pallas as pl
from jax.experimental.pallas import tpu as pltpu
from jax.sharding import PartitionSpec as P

ROUNDS = 4
WIDTH = 256
PIECES = 2
AHEAD = 3


def unit_order(sections):
    order = []
    for number in range(ROUNDS):
        ks = list(range(sections))
        if number % 2 == 0:
            ks = ks[::-1]
        order += [(number, k) for k in ks]
    return order


def strip_kernel(nsec, count, chunks, width, *refs):
    owners_ref, x_ref, bank_ref, out_ref = refs[:4]
    xs, sa, sb, rs, ghi, glo, raw, names, named, ahi, alo, table_ref = refs[4:16]
    sections = bank_ref.shape[1]
    order = unit_order(sections)
    units = len(order)
    held = refs[16 : 17 + units]
    (x_sems, own_sem, line_sends, line_sems, pair_sem, far_send, far_sems, relay_send, relay_sems) = refs[17 + units : 26 + units]
    (row_sends, row_sems, return_sem, raw_sends, raw_sems, table_sem) = refs[26 + units :]

    extent = bank_ref.shape[3]
    half = extent // 2
    rows = bank_ref.shape[2]
    local_rows = sections * extent
    chips = count // 2
    sec = lax.axis_index("sec")
    me = lax.axis_index("col")
    chip, core = me // 2, me % 2
    partner = chip * 2 + 1 - core
    after = lax.rem(sec + 1, nsec)
    before = lax.rem(sec + nsec - 1, nsec)

    def columns(c):
        return pl.ds(pl.multiple_of(c * width, width), width)

    def load(c, k):
        return pltpu.make_async_copy(
            x_ref.at[pl.ds(k * extent, extent), columns(c)],
            xs.at[c, pl.ds(half + k * extent, extent)],
            x_sems.at[k],
        )

    def own(u):
        number, k = order[u]
        return pltpu.make_async_copy(bank_ref.at[number, k], held[u].at[core, chip], own_sem)

    barrier = pltpu.get_barrier_semaphore()

    def greet(target):
        pl.semaphore_signal(barrier, inc=1, device_id=target, device_id_type=pl.DeviceIdType.MESH)

    has_up, has_down = chip + 1 < chips, chip > 0
    greet({"sec": after})
    greet({"sec": before})
    greet({"col": partner})
    pl.when(has_up)(lambda: greet({"col": (chip + 1) * 2 + core}))
    pl.when(has_down)(lambda: greet({"col": (chip - 1) * 2 + core}))
    table = pltpu.make_async_copy(owners_ref, table_ref, table_sem)
    table.start()
    for k in range(sections - 1, -1, -1):
        lax.fori_loop(0, chunks, lambda c, _, k=k: (load(c, k).start(), 0)[1], 0)
    for u in range(units):
        own(u).start()
    pl.semaphore_wait(barrier, 3 + has_up.astype(jnp.int32) + has_down.astype(jnp.int32))

    def settle(ref, sem):
        pltpu.make_async_copy(ref, ref, sem).wait()

    def settle_blocks(blocks, sem):
        settle(sb.at[:, pl.ds(0, blocks * rows * extent // (chunks * width))], sem)

    def remote(src, dst, send_sem, recv_sem, target):
        return pltpu.make_async_remote_copy(
            src_ref=src,
            dst_ref=dst,
            send_sem=send_sem,
            recv_sem=recv_sem,
            device_id=target,
            device_id_type=pl.DeviceIdType.MESH,
        )

    early = chunks - 1
    last = sections - 1
    extra = units

    def raw_block():
        return remote(bank_ref.at[0, last], held[extra].at[core, chip], raw_sends.at[0], raw_sems.at[0], {"sec": after})

    def raw_names():
        return remote(names, named, raw_sends.at[1], raw_sems.at[1], {"sec": after})

    def raw_rows():
        return remote(
            x_ref.at[pl.ds(last * extent, extent), pl.ds(early * width, width)],
            raw,
            raw_sends.at[2],
            raw_sems.at[2],
            {"sec": after},
        )

    raw_block().start()
    pl.when(core == 0)(lambda: raw_rows().start())

    part = rows // PIECES
    first_number, first_k = order[0]

    def piece(p):
        return pl.ds(p * part, part)

    def passed(src, slot, p, way, target):
        return remote(src, held[0].at[core, slot, piece(p)], line_sends.at[way], line_sems.at[slot, p], {"col": target})

    def pass_up(src, slot, p):
        return passed(src, slot, p, 0, (chip + 1) * 2 + core)

    def pass_down(src, slot, p):
        return passed(src, slot, p, 1, (chip - 1) * 2 + core)

    def pass_pair(src, slot, p):
        return remote(src, held[0].at[core, slot, piece(p)], line_sends.at[2], pair_sem, {"col": partner})

    def own_piece(p):
        return bank_ref.at[first_number, first_k, piece(p)]

    for p in range(PIECES):
        pl.when(has_up)(lambda p=p: pass_up(own_piece(p), chip, p).start())
        pl.when(has_down)(lambda p=p: pass_down(own_piece(p), chip, p).start())
    for p in range(PIECES):
        pass_pair(own_piece(p), chip, p).start()
    for step in range(chips - 1):
        low, high = chip - 1 - step, chip + 1 + step
        for p in range(PIECES):

            @pl.when(low >= 0)
            def _(step=step, p=p, low=low):
                src = held[0].at[core, low, piece(p)]
                pass_up(src, low, p).wait_recv()
                if step + 1 < chips - 1:
                    pl.when(has_up)(lambda: pass_up(src, low, p).start())
                pass_pair(src, low, p).start()

            @pl.when(high < chips)
            def _(step=step, p=p, high=high):
                src = held[0].at[core, high, piece(p)]
                pass_down(src, high, p).wait_recv()
                if step + 1 < chips - 1:
                    pl.when(has_down)(lambda: pass_down(src, high, p).start())
                pass_pair(src, high, p).start()

            if step == 0 and p == 0:
                pl.when(core == 1)(lambda: raw_rows().start())

    table.wait()
    for p in range(count):
        names[p : p + 1, :] = jnp.full((1, extent), table_ref[0, last, p].astype(jnp.float32))
    raw_names().start()

    def far(u, d):
        return remote(
            held[extra].at[core, chip] if u == extra else bank_ref.at[order[u]],
            held[u].at[core, chip],
            far_send,
            far_sems.at[u - 1],
            {"col": lax.rem(chip + d, chips) * 2 + core},
        )

    turns = []

    def relay(u, side):
        at = turns.index(u) % 2
        return remote(held[u].at[side], held[u].at[side], relay_send, relay_sems.at[at], {"col": partner})

    def order_rows(u):
        number, k = order[u]
        for b in range(count):
            place = jnp.int32(0)
            for c in range(count):
                place = jnp.where(table_ref[number, k, c] == b, c, place)
            block = held[u][place % 2, place // 2]
            high = block.astype(jnp.bfloat16)
            ghi[u, b * rows : (b + 1) * rows, :] = high
            glo[u, b * rows : (b + 1) * rows, :] = (block - high.astype(jnp.float32)).astype(jnp.bfloat16)

    settle(bank_ref, own_sem)
    settle(held[0].at[1 - core], pair_sem)
    order_rows(0)

    def collect(u):
        turns.append(u)
        settle(held[u].at[core, pl.ds(0, chips - 1)], far_sems.at[u - 1])
        relay(u, core).start()
        relay(u, 1 - core).wait_recv()

    def receive(u):
        collect(u)
        order_rows(u)

    def split(value):
        high = value.astype(jnp.bfloat16)
        return high, (value - high.astype(jnp.float32)).astype(jnp.bfloat16)

    def product(u, begin, size, parts):
        high, low = parts
        a, b = ghi[u, begin : begin + size, :], glo[u, begin : begin + size, :]
        dot = functools.partial(jnp.dot, preferred_element_type=jnp.float32)
        return dot(a, high) + (dot(a, low) + dot(b, high))

    index = {pair: u for u, pair in enumerate(order)}
    top = half + local_rows

    def forward(c, which, buf):
        return remote(
            buf.at[c, pl.ds(top - half, half)],
            buf.at[c, pl.ds(0, half)],
            row_sends.at[which],
            row_sems.at[0, c],
            {"sec": after},
        )

    def back_first(c):
        return remote(
            rs.at[c],
            sb.at[c, pl.ds(local_rows - half, half)],
            row_sends.at[1],
            row_sems.at[1, c],
            {"sec": before},
        )

    def back_last(c):
        return remote(
            sa.at[c, pl.ds(0, half)],
            out_ref.at[pl.ds(local_rows - half, half), columns(c)],
            row_sends.at[3],
            return_sem,
            {"sec": before},
        )

    def each_chunk(body, start=0, stop=chunks):
        lax.fori_loop(start, stop, lambda c, _: (body(c), 0)[1], 0)


    settle(xs.at[:, pl.ds(half + last * extent, extent)], x_sems.at[last])

    def begin(c):
        parts = split(xs[c, half + last * extent : top])
        u = index[0, last]
        sa[c, top - half : top] = product(u, half, half, parts)
        pl.when((c == 1) & (core == 1))(lambda: forward(0, 0, sa).start())
        pl.when((c != early) & ((c > 0) | (core == 0)))(lambda: forward(c, 0, sa).start())
        sa[c, half + last * extent : top - half] = product(u, 0, half, parts)

    def send_far(*chosen):
        for u in chosen:
            for d in range(1, chips):
                far(u, d).start()

    each_chunk(begin, 0, AHEAD)
    send_far(1, 2)
    each_chunk(begin, AHEAD)
    raw_block().wait_recv()
    send_far(extra, *range(3, units))

    for k in range(last - 1, -1, -1):
        receive(index[0, k])
        settle(xs.at[:, pl.ds(half + k * extent, extent)], x_sems.at[k])

        def inner(c, k=k):
            at = half + k * extent
            parts = split(xs[c, at : at + extent])
            sa[c, at : at + extent] = product(index[0, k], 0, extent, parts)

        each_chunk(inner)

    receive(index[1, 0])

    def straddle(c):
        pl.when(c != early)(lambda: forward(c, 0, sa).wait_recv())
        parts = split(sa[c, 0:extent])
        u = index[1, 0]
        rs[c] = product(u, 0, half, parts)
        back_first(c).start()
        sb[c, 0:half] = product(u, half, half, parts)

    each_chunk(straddle, stop=early)

    collect(extra)
    raw_names().wait_recv()
    raw_rows().wait_recv()
    for b in range(count // 2, count):
        block = jnp.zeros((rows, extent), jnp.float32)
        for p in range(count):
            number_of = jnp.broadcast_to(named[p : p + 1, :], (rows, extent))
            block = jnp.where(number_of == float(b), held[extra][p % 2, p // 2], block)
        at = (b - count // 2) * rows
        ahi[at : at + rows, :], alo[at : at + rows, :] = split(block)
    dot = functools.partial(jnp.dot, preferred_element_type=jnp.float32)
    high, low = split(raw[...])
    sa[early, 0:half] = dot(ahi[...], high) + (dot(ahi[...], low) + dot(alo[...], high))
    straddle(early)
    for k in range(1, sections):
        receive(index[1, k])

        def inner(c, k=k):
            parts = split(sa[c, k * extent : (k + 1) * extent])
            sb[c, k * extent - half : (k + 1) * extent - half] = product(index[1, k], 0, extent, parts)

        each_chunk(inner)

    for k in range(last, -1, -1):
        receive(index[2, k])

    def middle(c):
        back_first(c).wait_recv()
        parts = split(sb[c, last * extent : local_rows])
        u = index[2, last]
        xs[c, top - half : top] = product(u, half, half, parts)
        forward(c, 2, xs).start()
        xs[c, half + last * extent : top - half] = product(u, 0, half, parts)
        for k in range(last):
            at = half + k * extent
            parts = split(sb[c, k * extent : (k + 1) * extent])
            xs[c, at : at + extent] = product(index[2, k], 0, extent, parts)

    each_chunk(middle)

    for k in range(sections):
        receive(index[3, k])

    def finish(c):
        forward(c, 2, xs).wait_recv()
        parts = split(xs[c, 0:extent])
        u = index[3, 0]
        sa[c, 0:half] = product(u, 0, half, parts)
        back_last(c).start()
        out_ref[0:half, columns(c)] = product(u, half, half, parts)
        for k in range(1, sections):
            parts = split(xs[c, k * extent : (k + 1) * extent])
            out_ref[k * extent - half : (k + 1) * extent - half, columns(c)] = product(
                index[3, k], 0, extent, parts
            )

    each_chunk(finish)

    for v in range(chips):
        if v + 1 < chips:
            pl.when(chip == v)(lambda: settle(held[0].at[core, pl.ds(0, v + 1)], line_sends.at[0]))
        if v > 0:
            pl.when(chip == v)(lambda: settle(held[0].at[core, pl.ds(0, chips - v)], line_sends.at[1]))
    settle(held[0].at[core], line_sends.at[2])
    settle_blocks(units * (chips - 1), far_send)
    settle_blocks(units * chips, relay_send)
    raw_block().wait_send()
    raw_names().wait_send()
    raw_rows().wait_send()
    if early:
        settle(sa.at[pl.ds(0, early), pl.ds(top - half, half)], row_sends.at[0])
    settle(rs, row_sends.at[1])
    settle(xs.at[:, pl.ds(top - half, half)], row_sends.at[2])
    settle(sa.at[:, pl.ds(0, half)], row_sends.at[3])
    settle(out_ref.at[pl.ds(local_rows - half, half)], return_sem)


def local(matrix_rows, factor_bank, owner_table):
    nsec, count = lax.axis_size("sec"), lax.axis_size("col")
    sections, rows, extent = factor_bank.shape[1:]
    local_rows, columns = matrix_rows.shape
    half, chips = extent // 2, count // 2
    width = WIDTH if columns % WIDTH == 0 else columns
    chunks = columns // width
    units = ROUNDS * sections
    f32, bf16, dma = jnp.float32, jnp.bfloat16, pltpu.SemaphoreType.DMA
    return pl.pallas_call(
        functools.partial(strip_kernel, nsec, count, chunks, width),
        out_shape=pltpu.VMEM(matrix_rows.shape, matrix_rows.dtype),
        in_specs=[
            pl.BlockSpec(memory_space=pl.ANY),
            pl.BlockSpec(memory_space=pl.ANY),
            pl.BlockSpec(memory_space=pl.ANY),
        ],
        out_specs=pl.BlockSpec(memory_space=pltpu.VMEM),
        scratch_shapes=[
            pltpu.VMEM((chunks, half + local_rows, width), f32),
            pltpu.VMEM((chunks, half + local_rows, width), f32),
            pltpu.VMEM((chunks, local_rows, width), f32),
            pltpu.VMEM((chunks, half, width), f32),
            pltpu.VMEM((units, extent, extent), bf16),
            pltpu.VMEM((units, extent, extent), bf16),
            pltpu.VMEM((extent, width), f32),
            pltpu.VMEM((count, extent), f32),
            pltpu.VMEM((count, extent), f32),
            pltpu.VMEM((half, extent), bf16),
            pltpu.VMEM((half, extent), bf16),
            pltpu.SMEM((ROUNDS, sections, count), jnp.int32),
            *[pltpu.VMEM((2, chips, rows, extent), f32) for _ in range(units + 1)],
            dma((sections,)),
            dma(()),
            dma((3,)),
            dma((chips, PIECES)),
            dma(()),
            dma(()),
            dma((units,)),
            dma(()),
            dma((2,)),
            dma((4,)),
            dma((2, chunks)),
            dma(()),
            dma((3,)),
            dma((3,)),
            dma(()),
        ],
        compiler_params=pltpu.CompilerParams(
            collective_id=0, has_side_effects=True, vmem_limit_bytes=54 << 20
        ),
        name="strip",
    )(owner_table, matrix_rows, factor_bank)


def solution(mesh):
    in_specs = (P("sec", "col"), P(None, "sec", "col", None), P(None, "sec", None))
    out_specs = P("sec", "col")
    return jax.shard_map(local, mesh=mesh, in_specs=in_specs, out_specs=out_specs, check_vma=False)
```

```python
import functools

import jax
import jax.numpy as jnp
from jax import lax
from jax.experimental import pallas as pl
from jax.experimental.pallas import tpu as pltpu
from jax.sharding import PartitionSpec as P

ROUNDS = 4
WIDTH = 256
PIECES = 2
AHEAD = 3


def unit_order(sections):
    order = []
    for number in range(ROUNDS):
        ks = list(range(sections))
        if number % 2 == 0:
            ks = ks[::-1]
        order += [(number, k) for k in ks]
    return order


def strip_kernel(nsec, count, chunks, width, *refs):
    owners_ref, x_ref, bank_ref, out_ref = refs[:4]
    xs, sa, sb, rs, ghi, glo, raw, names, named, ahi, alo, table_ref = refs[4:16]
    sections = bank_ref.shape[1]
    order = unit_order(sections)
    units = len(order)
    held = refs[16 : 17 + units]
    (x_sems, own_sem, line_sends, line_sems, pair_sem, far_send, far_sems, relay_sems) = refs[17 + units : 25 + units]
    (row_send, row_sems, return_sem, raw_sems, table_sem) = refs[25 + units :]

    extent = bank_ref.shape[3]
    half = extent // 2
    rows = bank_ref.shape[2]
    local_rows = sections * extent
    chips = count // 2
    sec = lax.axis_index("sec")
    me = lax.axis_index("col")
    chip, core = me // 2, me % 2
    partner = chip * 2 + 1 - core
    after = lax.rem(sec + 1, nsec)
    before = lax.rem(sec + nsec - 1, nsec)

    def columns(c):
        return pl.ds(pl.multiple_of(c * width, width), width)

    def load(c, k):
        return pltpu.make_async_copy(
            x_ref.at[pl.ds(k * extent, extent), columns(c)],
            xs.at[c, pl.ds(half + k * extent, extent)],
            x_sems.at[k],
        )

    def own(u):
        number, k = order[u]
        return pltpu.make_async_copy(bank_ref.at[number, k], held[u].at[core, chip], own_sem)

    barrier = pltpu.get_barrier_semaphore()

    def greet(target):
        pl.semaphore_signal(barrier, inc=1, device_id=target, device_id_type=pl.DeviceIdType.MESH)

    has_up, has_down = chip + 1 < chips, chip > 0
    greet({"sec": after})
    greet({"sec": before})
    greet({"col": partner})
    pl.when(has_up)(lambda: greet({"col": (chip + 1) * 2 + core}))
    pl.when(has_down)(lambda: greet({"col": (chip - 1) * 2 + core}))
    table = pltpu.make_async_copy(owners_ref, table_ref, table_sem)
    table.start()
    for k in range(sections - 1, -1, -1):
        lax.fori_loop(0, chunks, lambda c, _, k=k: (load(c, k).start(), 0)[1], 0)
    for u in range(units):
        own(u).start()
    pl.semaphore_wait(barrier, 3 + has_up.astype(jnp.int32) + has_down.astype(jnp.int32))

    def settle(ref, sem):
        pltpu.make_async_copy(ref, ref, sem).wait()

    def settle_blocks(blocks, sem):
        settle(sb.at[:, pl.ds(0, blocks * rows * extent // (chunks * width))], sem)

    def remote(src, dst, send_sem, recv_sem, target):
        return pltpu.make_async_remote_copy(
            src_ref=src,
            dst_ref=dst,
            send_sem=send_sem,
            recv_sem=recv_sem,
            device_id=target,
            device_id_type=pl.DeviceIdType.MESH,
        )

    early = chunks - 1
    last = sections - 1
    extra = units

    def raw_block():
        return remote(bank_ref.at[0, last], held[extra].at[core, chip], row_send, raw_sems.at[0], {"sec": after})

    def raw_names():
        return remote(names, named, table_sem, raw_sems.at[1], {"sec": after})

    def raw_rows():
        return remote(
            x_ref.at[pl.ds(last * extent, extent), pl.ds(early * width, width)],
            raw,
            row_send,
            raw_sems.at[2],
            {"sec": after},
        )

    raw_block().start()
    pl.when(core == 0)(lambda: raw_rows().start())

    part = rows // PIECES
    first_number, first_k = order[0]

    def piece(p):
        return pl.ds(p * part, part)

    def passed(src, slot, p, way, target):
        return remote(src, held[0].at[core, slot, piece(p)], line_sends.at[way], line_sems.at[slot, p], {"col": target})

    def pass_up(src, slot, p):
        return passed(src, slot, p, 0, (chip + 1) * 2 + core)

    def pass_down(src, slot, p):
        return passed(src, slot, p, 1, (chip - 1) * 2 + core)

    def pass_pair(src, slot, p):
        return remote(src, held[0].at[core, slot, piece(p)], line_sends.at[2], pair_sem, {"col": partner})

    def own_piece(p):
        return bank_ref.at[first_number, first_k, piece(p)]

    for p in range(PIECES):
        pl.when(has_up)(lambda p=p: pass_up(own_piece(p), chip, p).start())
        pl.when(has_down)(lambda p=p: pass_down(own_piece(p), chip, p).start())
    for p in range(PIECES):
        pass_pair(own_piece(p), chip, p).start()
    for step in range(chips - 1):
        low, high = chip - 1 - step, chip + 1 + step
        for p in range(PIECES):

            @pl.when(low >= 0)
            def _(step=step, p=p, low=low):
                src = held[0].at[core, low, piece(p)]
                pass_up(src, low, p).wait_recv()
                if step + 1 < chips - 1:
                    pl.when(has_up)(lambda: pass_up(src, low, p).start())
                pass_pair(src, low, p).start()

            @pl.when(high < chips)
            def _(step=step, p=p, high=high):
                src = held[0].at[core, high, piece(p)]
                pass_down(src, high, p).wait_recv()
                if step + 1 < chips - 1:
                    pl.when(has_down)(lambda: pass_down(src, high, p).start())
                pass_pair(src, high, p).start()

            if step == 0 and p == 0:
                pl.when(core == 1)(lambda: raw_rows().start())

    table.wait()
    for p in range(count):
        names[p : p + 1, :] = jnp.full((1, extent), table_ref[0, last, p].astype(jnp.float32))
    raw_names().start()

    def far(u, d):
        return remote(
            held[extra].at[core, chip] if u == extra else bank_ref.at[order[u]],
            held[u].at[core, chip],
            far_send,
            far_sems.at[u - 1],
            {"col": lax.rem(chip + d, chips) * 2 + core},
        )

    turns = []

    def relay(u, side):
        at = turns.index(u) % 2
        return remote(held[u].at[side], held[u].at[side], far_send, relay_sems.at[at], {"col": partner})

    def order_rows(u):
        number, k = order[u]
        for b in range(count):
            place = jnp.int32(0)
            for c in range(count):
                place = jnp.where(table_ref[number, k, c] == b, c, place)
            block = held[u][place % 2, place // 2]
            high = block.astype(jnp.bfloat16)
            ghi[u, b * rows : (b + 1) * rows, :] = high
            glo[u, b * rows : (b + 1) * rows, :] = (block - high.astype(jnp.float32)).astype(jnp.bfloat16)

    settle(bank_ref, own_sem)
    settle(held[0].at[1 - core], pair_sem)
    order_rows(0)

    def collect(u):
        turns.append(u)
        settle(held[u].at[core, pl.ds(0, chips - 1)], far_sems.at[u - 1])
        relay(u, core).start()
        relay(u, 1 - core).wait_recv()

    def receive(u):
        collect(u)
        order_rows(u)

    def split(value):
        high = value.astype(jnp.bfloat16)
        return high, (value - high.astype(jnp.float32)).astype(jnp.bfloat16)

    def product(u, begin, size, parts):
        high, low = parts
        a, b = ghi[u, begin : begin + size, :], glo[u, begin : begin + size, :]
        dot = functools.partial(jnp.dot, preferred_element_type=jnp.float32)
        return dot(a, high) + (dot(a, low) + dot(b, high))

    index = {pair: u for u, pair in enumerate(order)}
    top = half + local_rows

    def forward(c, which, buf):
        return remote(
            buf.at[c, pl.ds(top - half, half)],
            buf.at[c, pl.ds(0, half)],
            row_send,
            row_sems.at[0, c],
            {"sec": after},
        )

    def back_first(c):
        return remote(
            rs.at[c],
            sb.at[c, pl.ds(local_rows - half, half)],
            row_send,
            row_sems.at[1, c],
            {"sec": before},
        )

    def back_last(c):
        return remote(
            sa.at[c, pl.ds(0, half)],
            out_ref.at[pl.ds(local_rows - half, half), columns(c)],
            row_send,
            return_sem,
            {"sec": before},
        )

    def each_chunk(body, start=0, stop=chunks):
        lax.fori_loop(start, stop, lambda c, _: (body(c), 0)[1], 0)


    settle(xs.at[:, pl.ds(half + last * extent, extent)], x_sems.at[last])

    def begin(c):
        parts = split(xs[c, half + last * extent : top])
        u = index[0, last]
        sa[c, top - half : top] = product(u, half, half, parts)
        pl.when((c == 1) & (core == 1))(lambda: forward(0, 0, sa).start())
        pl.when((c != early) & ((c > 0) | (core == 0)))(lambda: forward(c, 0, sa).start())
        sa[c, half + last * extent : top - half] = product(u, 0, half, parts)

    def send_far(*chosen):
        for u in chosen:
            for d in range(1, chips):
                far(u, d).start()

    each_chunk(begin, 0, AHEAD)
    send_far(1, 2)
    each_chunk(begin, AHEAD)
    raw_block().wait_recv()
    send_far(extra, *range(3, units))

    for k in range(last - 1, -1, -1):
        receive(index[0, k])
        settle(xs.at[:, pl.ds(half + k * extent, extent)], x_sems.at[k])

        def inner(c, k=k):
            at = half + k * extent
            parts = split(xs[c, at : at + extent])
            sa[c, at : at + extent] = product(index[0, k], 0, extent, parts)

        each_chunk(inner)

    receive(index[1, 0])

    def straddle(c):
        pl.when(c != early)(lambda: forward(c, 0, sa).wait_recv())
        parts = split(sa[c, 0:extent])
        u = index[1, 0]
        rs[c] = product(u, 0, half, parts)
        back_first(c).start()
        sb[c, 0:half] = product(u, half, half, parts)

    each_chunk(straddle, stop=early)

    collect(extra)
    raw_names().wait_recv()
    raw_rows().wait_recv()
    for b in range(count // 2, count):
        block = jnp.zeros((rows, extent), jnp.float32)
        for p in range(count):
            number_of = jnp.broadcast_to(named[p : p + 1, :], (rows, extent))
            block = jnp.where(number_of == float(b), held[extra][p % 2, p // 2], block)
        at = (b - count // 2) * rows
        ahi[at : at + rows, :], alo[at : at + rows, :] = split(block)
    dot = functools.partial(jnp.dot, preferred_element_type=jnp.float32)
    high, low = split(raw[...])
    sa[early, 0:half] = dot(ahi[...], high) + (dot(ahi[...], low) + dot(alo[...], high))
    straddle(early)
    for k in range(1, sections):
        receive(index[1, k])

        def inner(c, k=k):
            parts = split(sa[c, k * extent : (k + 1) * extent])
            sb[c, k * extent - half : (k + 1) * extent - half] = product(index[1, k], 0, extent, parts)

        each_chunk(inner)

    for k in range(last, -1, -1):
        receive(index[2, k])

    def middle(c):
        back_first(c).wait_recv()
        parts = split(sb[c, last * extent : local_rows])
        u = index[2, last]
        xs[c, top - half : top] = product(u, half, half, parts)
        forward(c, 2, xs).start()
        xs[c, half + last * extent : top - half] = product(u, 0, half, parts)
        for k in range(last):
            at = half + k * extent
            parts = split(sb[c, k * extent : (k + 1) * extent])
            xs[c, at : at + extent] = product(index[2, k], 0, extent, parts)

    each_chunk(middle)

    for k in range(sections):
        receive(index[3, k])

    def finish(c):
        forward(c, 2, xs).wait_recv()
        parts = split(xs[c, 0:extent])
        u = index[3, 0]
        sa[c, 0:half] = product(u, 0, half, parts)
        back_last(c).start()
        out_ref[0:half, columns(c)] = product(u, half, half, parts)
        for k in range(1, sections):
            parts = split(xs[c, k * extent : (k + 1) * extent])
            out_ref[k * extent - half : (k + 1) * extent - half, columns(c)] = product(
                index[3, k], 0, extent, parts
            )

    each_chunk(finish)

    for v in range(chips):
        if v + 1 < chips:
            pl.when(chip == v)(lambda: settle(held[0].at[core, pl.ds(0, v + 1)], line_sends.at[0]))
        if v > 0:
            pl.when(chip == v)(lambda: settle(held[0].at[core, pl.ds(0, chips - v)], line_sends.at[1]))
    settle(held[0].at[core], line_sends.at[2])
    settle_blocks(units * (2 * chips - 1), far_send)
    sent = (early + 3 * chunks) * half * width + (rows + width) * extent
    settle(xs.at[:, pl.ds(0, sent // (chunks * width))], row_send)
    raw_names().wait_send()
    settle(out_ref.at[pl.ds(local_rows - half, half)], return_sem)


def local(matrix_rows, factor_bank, owner_table):
    nsec, count = lax.axis_size("sec"), lax.axis_size("col")
    sections, rows, extent = factor_bank.shape[1:]
    local_rows, columns = matrix_rows.shape
    half, chips = extent // 2, count // 2
    width = WIDTH if columns % WIDTH == 0 else columns
    chunks = columns // width
    units = ROUNDS * sections
    f32, bf16, dma = jnp.float32, jnp.bfloat16, pltpu.SemaphoreType.DMA
    return pl.pallas_call(
        functools.partial(strip_kernel, nsec, count, chunks, width),
        out_shape=pltpu.VMEM(matrix_rows.shape, matrix_rows.dtype),
        in_specs=[
            pl.BlockSpec(memory_space=pl.ANY),
            pl.BlockSpec(memory_space=pl.ANY),
            pl.BlockSpec(memory_space=pl.ANY),
        ],
        out_specs=pl.BlockSpec(memory_space=pltpu.VMEM),
        scratch_shapes=[
            pltpu.VMEM((chunks, half + local_rows, width), f32),
            pltpu.VMEM((chunks, half + local_rows, width), f32),
            pltpu.VMEM((chunks, local_rows, width), f32),
            pltpu.VMEM((chunks, half, width), f32),
            pltpu.VMEM((units, extent, extent), bf16),
            pltpu.VMEM((units, extent, extent), bf16),
            pltpu.VMEM((extent, width), f32),
            pltpu.VMEM((count, extent), f32),
            pltpu.VMEM((count, extent), f32),
            pltpu.VMEM((half, extent), bf16),
            pltpu.VMEM((half, extent), bf16),
            pltpu.SMEM((ROUNDS, sections, count), jnp.int32),
            *[pltpu.VMEM((2, chips, rows, extent), f32) for _ in range(units + 1)],
            dma((sections,)),
            dma(()),
            dma((3,)),
            dma((chips, PIECES)),
            dma(()),
            dma(()),
            dma((units,)),
            dma((2,)),
            dma(()),
            dma((2, chunks)),
            dma(()),
            dma((3,)),
            dma(()),
        ],
        compiler_params=pltpu.CompilerParams(
            collective_id=0, has_side_effects=True, vmem_limit_bytes=54 << 20
        ),
        name="strip",
    )(owner_table, matrix_rows, factor_bank)


def solution(mesh):
    in_specs = (P("sec", "col"), P(None, "sec", "col", None), P(None, "sec", None))
    out_specs = P("sec", "col")
    return jax.shard_map(local, mesh=mesh, in_specs=in_specs, out_specs=out_specs, check_vma=False)
```
